32 devices in a mesh: grp: 4 (over y, x), sub: 8 (over z, core).
Axes of the slice: x: 2, y: 2, z: 4, core: 2. Of those that a mesh axis runs over, the one named last changes fastest.
Arguments:
- measurement_block_rows: bfloat16 [2048, 4, 1536], P(('grp', 'sub')), may hold values from -0.15625 to 0.15625
- measurement_residual: bfloat16 [2048, 4], P(('grp', 'sub')), may hold values from -6 to 6
- owner: int32 [2048, 1], P(('grp', 'sub')), may hold values from 0 to 7; in each aligned block of 64 rows (0 to 63, 64 to 127, ...) at most 16 rows name the same one
- submap_prior_weight: float32 [32, 1536], P(('grp', 'sub')), may hold values from 0.5 to 2
- separator_measure_rows: bfloat16 [32768, 1024], P(('grp', 'sub')), may hold values from -5 to 5
- separator_residual: bfloat16 [32, 1024], P(('grp', 'sub')), may hold values from -6 to 6
- separator_prior_weight: float32 [32, 1024], P(('grp', 'sub')), may hold values from 0.3 to 0.6
Outputs:
- interior_step: float32 [32, 1024], P(('grp', 'sub'))
- node_step: float32 [32, 512], P(('grp', 'sub'))
The draws below stay inside these ranges and needn't reach their ends.
Inputs may be any that keep to these rules, and one draw needn't show every extreme that they name: Among the 64 blocks of one device no owner is named more than 16 times; in every draw some device names some owner exactly 16 times.
All inputs are finite; a program needn't handle non-finite values.
Results may differ from the reference program's by a relative error of at most 0.0003.
Values may be sent and summed in bfloat16 or wider, within the bound.
A program may use at most 192 MiB of HBM per device.

```python
import math
import jax
import jax.numpy as jnp
import numpy as np
from jax import lax

NI = 1024
W = 512
SUBMAP_COLUMNS = 1536
BLOCK_ROW_COUNT = 4
BLOCKS_PER_UNIT = 64
CAP = 16
RN = 1024
N_GRP = 4
N_SUB = 8


def draw_separator_measure_rows(key, part):
    own_key = jax.random.fold_in(key, 11)
    jitter_key = jax.random.fold_in(key, 12)
    row_count = N_GRP * N_SUB * RN
    spread_scale = (16.0 / RN) ** 0.5
    own_half = jnp.clip(jax.random.normal(own_key, (row_count, W), jnp.float32), -6.0, 6.0)
    own_half = own_half * spread_scale
    jitter = jax.random.uniform(jitter_key, (row_count, W), jnp.float32, -0.1875, 0.1875) * spread_scale
    parent_half = own_half + jitter
    return jnp.concatenate([own_half, parent_half], axis=1).astype(jnp.bfloat16)


def shard_levels(stream_key, shape, cuts, low, high):
    level = 1.0
    for dim, parts in cuts:
        steps = jax.random.uniform(jax.random.fold_in(jax.random.fold_in(stream_key, 6), dim), (parts,), jnp.float32, low / len(cuts), high / len(cuts))
        level = level * jnp.repeat(jnp.exp(steps), shape[dim] // parts).reshape((-1,) + (1,) * (len(shape) - 1 - dim))
    return level


def routed_block(key, own, number, rows, number_of, top, reach, slope):
    ranking = jax.random.permutation(key, number_of)
    packed, usual = load_shares(number_of, rows * top, reach, slope, True), load_shares(number_of, rows * top, reach, slope, False)
    places = jnp.arange(number_of)

    def named(tallies, turn):
        used = int((tallies > 0).sum())
        fixed = max(1, used // 4)
        shifted = fixed + (places - fixed + turn * (used - fixed)) % max(1, number_of - fixed)
        return jnp.zeros((number_of,), jnp.int32).at[ranking[jnp.where(places < fixed, places, shifted)]].set(jnp.asarray(tallies, jnp.int32))

    tallies = jnp.where(number % 4 == 0, named(packed, number // 4), named(usual, number - number // 4 - 1))
    mixed = jax.random.permutation(jax.random.fold_in(own, 3), number_of)
    donor, sink = mixed[0:number_of // 2 * 2:2], mixed[1:number_of // 2 * 2:2]
    slack = jnp.minimum(tallies[donor] - 1, reach - tallies[sink]) // 2
    slack = jnp.where((donor == ranking[0]) | (sink == ranking[0]) | (tallies[sink] == 0), 0, jnp.maximum(slack, 0))
    shifted = jax.random.randint(jax.random.fold_in(own, 4), (number_of // 2,), 0, 1 << 20) % (slack + 1)
    tallies = tallies.at[donor].add(-shifted).at[sink].add(shifted)
    members = jnp.searchsorted(jnp.cumsum(tallies), jnp.arange(rows * top), side="right").astype(jnp.int32)
    grid = members.reshape(top, rows).T
    grid = grid[jax.random.permutation(jax.random.fold_in(own, 1), rows)]
    turn = jax.random.randint(jax.random.fold_in(own, 2), (rows, 1), 0, top)
    return jnp.take_along_axis(grid, (jnp.arange(top)[None, :] + turn) % top, axis=1)


def load_shares(number_of, total, bound, slope, full):
    loads = [(1 << 20) // math.isqrt(grade ** slope) + 1 for grade in range(1, number_of + 1)]
    largest = bound if full else min(bound, max(-(-total // number_of), total * loads[0] // sum(loads)))
    least = 1 if total - largest >= number_of - 1 else 0
    holding, spare = [largest] + [least] * (number_of - 1), total - largest - least * (number_of - 1)
    while spare > 0:
        movable = [i for i in range(1, number_of) if holding[i] < largest] or [i for i in range(1, number_of) if holding[i] < bound]
        pool, remaining = sum([loads[i] for i in movable]), spare
        for i in movable:
            more = min(bound - holding[i], max(1, remaining * loads[i] // pool), spare)
            holding[i] = holding[i] + more
            spare = spare - more
    return np.array(holding)


def scatter_about(stream_key, extent, width, most, cuts=(), held_as=jnp.bfloat16):
    entries = jax.random.normal(stream_key, extent, jnp.float32) * width
    if len(cuts) > 0:
        entries = shard_levels(stream_key, extent, cuts, -0.22, 0.18) * entries
    return jnp.clip(entries, min=-most, max=most).astype(held_as)


def setup_inputs(seed: int = 0) -> dict:
    arg_keys = jax.random.split(jax.random.key(seed), 8)
    measurement_block_rows = scatter_about(arg_keys[0], (BLOCKS_PER_UNIT * N_GRP * N_SUB, BLOCK_ROW_COUNT, SUBMAP_COLUMNS), SUBMAP_COLUMNS ** -0.5, 0.15625, ((0, 32),))
    measurement_residual = scatter_about(arg_keys[1], (BLOCKS_PER_UNIT * N_GRP * N_SUB, BLOCK_ROW_COUNT), 1.0, 6.0, ((0, 32),))
    owner_keys = jax.random.split(jax.random.fold_in(arg_keys[2], 1), (BLOCKS_PER_UNIT * N_GRP * N_SUB) // BLOCKS_PER_UNIT)
    owner_turns = jax.random.permutation(jax.random.fold_in(arg_keys[2], 3), (BLOCKS_PER_UNIT * N_GRP * N_SUB) // BLOCKS_PER_UNIT)
    owner = jax.vmap(lambda own, number: routed_block(jax.random.fold_in(arg_keys[2], 2), own, number, BLOCKS_PER_UNIT, N_SUB, 1, CAP, 2))(owner_keys, owner_turns).reshape((BLOCKS_PER_UNIT * N_GRP * N_SUB, 1))
    submap_prior_weight = jnp.clip(jnp.exp(math.log(2.0) - 1.3862944 * jax.random.uniform(arg_keys[3], (N_GRP * N_SUB, SUBMAP_COLUMNS), jnp.float32) ** shard_levels(arg_keys[3], (N_GRP * N_SUB, SUBMAP_COLUMNS), ((0, 32),), -0.2, 0.2)), 0.5, 2.0)
    separator_measure_rows = draw_separator_measure_rows(jax.random.fold_in(arg_keys[7], 71), 0)
    separator_residual = scatter_about(arg_keys[5], (N_GRP * N_SUB, RN), 1.0, 6.0, ((0, 32),))
    separator_prior_weight = jnp.clip(jnp.exp(math.log(0.6) - 0.6931472 * jax.random.uniform(arg_keys[6], (N_GRP * N_SUB, 2 * W), jnp.float32) ** shard_levels(arg_keys[6], (N_GRP * N_SUB, 2 * W), ((0, 32),), -0.2, 0.2)), 0.3, 0.6)
    return dict(measurement_block_rows=measurement_block_rows, measurement_residual=measurement_residual, owner=owner, submap_prior_weight=submap_prior_weight, separator_measure_rows=separator_measure_rows, separator_residual=separator_residual, separator_prior_weight=separator_prior_weight)


highest = lax.Precision.HIGHEST

def eliminate(system, right_side, own_cols):
    factor = jnp.linalg.cholesky(system[:own_cols, :own_cols])
    coupled = jax.scipy.linalg.solve_triangular(factor, system[:own_cols, own_cols:], lower=True)
    reduced = jax.scipy.linalg.solve_triangular(factor, right_side[:own_cols], lower=True)
    schur_part = system[own_cols:, own_cols:] - jnp.dot(coupled.T, coupled, precision=highest)
    carried = right_side[own_cols:] - jnp.dot(coupled.T, reduced, precision=highest)
    back_shift = jax.scipy.linalg.solve_triangular(factor, reduced, lower=True, trans=1)
    back_gain = jax.scipy.linalg.solve_triangular(factor, coupled, lower=True, trans=1)
    return (schur_part, carried, back_shift, back_gain)

def slot_table(owner, device_count):
    owners = owner[:, 0].reshape(device_count, BLOCKS_PER_UNIT)
    onehot_own = (owners[:, :, None] == jnp.arange(N_SUB, dtype=jnp.int32)[None, None, :]).astype(jnp.int32)
    earlier = jnp.cumsum(onehot_own, axis=1) - onehot_own
    slot_rank = jnp.sum(earlier * onehot_own, axis=2)
    source = jnp.arange(device_count, dtype=jnp.int32)[:, None]
    target = source // N_SUB * N_SUB + owners
    position = target * (N_SUB * CAP) + source % N_SUB * CAP + slot_rank
    slot_index = jnp.full((device_count * N_SUB * CAP,), device_count * BLOCKS_PER_UNIT, jnp.int32)
    slot_index = slot_index.at[position.reshape(-1)].set(jnp.arange(device_count * BLOCKS_PER_UNIT, dtype=jnp.int32))
    return slot_index.reshape(device_count, N_SUB * CAP)

def reference(measurement_block_rows, measurement_residual, owner, submap_prior_weight, separator_measure_rows, separator_residual, separator_prior_weight):
    device_count = N_GRP * N_SUB
    tree_depth = device_count.bit_length() - 1
    slot_index = slot_table(owner, device_count)
    rows_padded = jnp.concatenate([measurement_block_rows, jnp.zeros((1, BLOCK_ROW_COUNT, SUBMAP_COLUMNS), measurement_block_rows.dtype)], axis=0)
    residual_padded = jnp.concatenate([measurement_residual, jnp.zeros((1, BLOCK_ROW_COUNT), measurement_residual.dtype)], axis=0)

    def leaf_one(item_args):
        index_row, prior_row = item_args
        row_block = rows_padded[index_row].reshape(-1, SUBMAP_COLUMNS).astype(jnp.float32)
        values = residual_padded[index_row].reshape(-1).astype(jnp.float32)
        system = jnp.einsum('rc,rd->cd', row_block, row_block, precision=highest) + jnp.diag(prior_row)
        right_side = jnp.einsum('rc,r->c', row_block, values, precision=highest)
        return eliminate(system, right_side, NI)
    leaf_schur, leaf_carry, leaf_shift, leaf_gain = lax.map(leaf_one, (slot_index, submap_prior_weight))
    node_mats = separator_measure_rows.reshape(device_count, RN, 2 * W)

    def node_one(item_args):
        host_id, extra_schur, extra_carry = item_args
        row_block = node_mats[host_id].astype(jnp.float32)
        values = separator_residual[host_id].astype(jnp.float32)
        system = jnp.einsum('rc,rd->cd', row_block, row_block, precision=highest) + jnp.diag(separator_prior_weight[host_id])
        right_side = jnp.einsum('rc,r->c', row_block, values, precision=highest)
        system = system.at[:W, :W].add(extra_schur)
        right_side = right_side.at[:W].add(extra_carry)
        return eliminate(system, right_side, W)
    node_schur = jnp.zeros((device_count, W, W), jnp.float32)
    node_carry = jnp.zeros((device_count, W), jnp.float32)
    node_shift = jnp.zeros((device_count, W), jnp.float32)
    node_gain = jnp.zeros((device_count, W, W), jnp.float32)
    for tree_level in range(1, tree_depth + 2):
        host_ids = jnp.arange(2 ** (tree_level - 1) - 1, device_count, 2 ** tree_level, dtype=jnp.int32)
        if tree_level == 1:
            extra_schur = leaf_schur[host_ids] + leaf_schur[host_ids + 1]
            extra_carry = leaf_carry[host_ids] + leaf_carry[host_ids + 1]
        else:
            stride = 2 ** (tree_level - 2)
            extra_schur = node_schur[host_ids - stride]
            extra_carry = node_carry[host_ids - stride]
            if tree_level <= tree_depth:
                extra_schur = extra_schur + node_schur[host_ids + stride]
                extra_carry = extra_carry + node_carry[host_ids + stride]
        schur_part, carried, back_shift, back_gain = lax.map(node_one, (host_ids, extra_schur, extra_carry))
        node_schur = node_schur.at[host_ids].set(schur_part)
        node_carry = node_carry.at[host_ids].set(carried)
        node_shift = node_shift.at[host_ids].set(back_shift)
        node_gain = node_gain.at[host_ids].set(back_gain)
    node_step = jnp.zeros((device_count, W), jnp.float32)
    for tree_level in range(tree_depth + 1, 0, -1):
        host_ids = jnp.arange(2 ** (tree_level - 1) - 1, device_count, 2 ** tree_level, dtype=jnp.int32)
        if tree_level == tree_depth + 1:
            parent_step = jnp.zeros((host_ids.shape[0], W), jnp.float32)
        else:
            is_left = (host_ids + 1) // 2 ** tree_level % 2 == 0
            parent_id = jnp.where(is_left, host_ids + 2 ** (tree_level - 1), host_ids - 2 ** (tree_level - 1))
            parent_step = node_step[parent_id]
        values = node_shift[host_ids] - jnp.einsum('hij,hj->hi', node_gain[host_ids], parent_step, precision=highest)
        node_step = node_step.at[host_ids].set(values)
    leaf_ids = jnp.arange(device_count, dtype=jnp.int32)
    frontier = node_step[leaf_ids - leaf_ids % 2]
    interior_step = leaf_shift - jnp.einsum('dij,dj->di', leaf_gain, frontier, precision=highest)
    return (interior_step, node_step)
```

```python
import jax
import jax.numpy as jnp
from jax import lax
from jax.experimental import pallas as pl
from jax.experimental.pallas import tpu as pltpu
from jax.sharding import PartitionSpec as P

NI = 1024
W = 512
B = 128
NB = W // B
QC = W + B
MESH = pl.DeviceIdType.MESH
highest = lax.Precision.HIGHEST


def mm(a, b, ca, cb):
    return lax.dot_general(
        a, b, (((ca,), (cb,)), ((), ())), precision=highest, preferred_element_type=jnp.float32
    )


def mm16(a, b, ca, cb):
    return lax.dot_general(a, b, (((ca,), (cb,)), ((), ())), preferred_element_type=jnp.float32)


def thirds(x):
    hi = x.astype(jnp.bfloat16)
    rest = x - hi.astype(jnp.float32)
    mid = rest.astype(jnp.bfloat16)
    low = (rest - mid.astype(jnp.float32)).astype(jnp.bfloat16)
    return hi, mid, low


def lane_spread(v, j):
    return jnp.broadcast_to(v[:, j:j + 1], (8, B))


def row_spread(v, i):
    return jnp.broadcast_to(v[i:i + 1, :], (8, B))


def pivot_pair(C, k):
    h, i = k // 8, k % 8
    X, Y = C[h][k], C[h][k + 1]
    a, b, c = row_spread(X, i), row_spread(X, i + 1), row_spread(Y, i + 1)
    r = 1.0 / (a * c - b * b)
    N, M = {}, {}
    for g in range(h, 2):
        Xg, Yg = C[g][k], C[g][k + 1]
        N[g] = (Xg * c - Yg * b, Yg * a - Xg * b)
        M[g] = (N[g][0] * r, N[g][1] * r)
    m = {}
    for j in range(k + 2, 16):
        hj = j // 8
        m[j] = (row_spread(M[hj][0], j % 8), row_spread(M[hj][1], j % 8))
        if j < k + 4:
            x, y = row_spread(C[hj][k], j % 8), row_spread(C[hj][k + 1], j % 8)
            for g in range(hj, 2):
                C[g][j] = C[g][j] - r * (N[g][0] * x + N[g][1] * y)
        else:
            for g in range(hj, 2):
                C[g][j] = C[g][j] - (C[g][k] * m[j][0] + C[g][k + 1] * m[j][1])
    return (a, b, c, r), m


def scaled_rows(u, pairs, sub):
    def join(parts, step):
        total = parts[0]
        for n in range(1, len(parts)):
            total = jnp.where(sub >= n * step, parts[n], total)
        return total

    a, b, r = (join([p[0][n] for p in pairs], 2) for n in (0, 1, 3))
    U, V = join(u, 1), join(u[0::2], 2)
    ra = lax.rsqrt(a)
    d = a * r
    return jnp.where(sub % 2 == 1, (U - (b * (ra * ra)) * V) * (d * lax.rsqrt(d)), U * ra)


def reduce_half(T, off):
    lane = lax.broadcasted_iota(jnp.int32, (8, B), 1)
    sub = lax.broadcasted_iota(jnp.int32, (8, B), 0)
    T = list(T)
    out = []
    n = len(T)
    for t in range(0, n, 2):
        la = off + 8 * t
        C = [[lane_spread(T[t], la + k) for k in range(8)],
             [lane_spread(T[t + 1], la + k) for k in range(16)]]
        cs = {i: [lane_spread(T[i], la + k) for k in range(8)] for i in range(t + 2, n)}
        cs[t + 1] = C[1][:8]
        pairs = [pivot_pair(C, k) for k in range(0, 16, 2)]
        for h in range(2):
            l = la + 8 * h
            inside = (lane >= l) & (lane < l + 8)
            base = jnp.where(inside, jnp.where(lane == sub + l, 1.0, 0.0), T[t + h])
            u = [row_spread(base, k) for k in range(8)]
            four = pairs[4 * h:4 * h + 4]
            for k in range(0, 6, 2):
                for i in range(k + 2, 8):
                    m = four[k // 2][1][i + 8 * h]
                    u[i] = u[i] - (m[0] * u[k] + m[1] * u[k + 1])
            out.append(scaled_rows(u, four, sub))
            if t + h + 1 == n:
                break
            q = [None] * 8
            for k in range(6, -1, -2):
                a, b, c, r = four[k // 2][0]
                q[k] = (c * u[k] - b * u[k + 1]) * r
                q[k + 1] = (a * u[k + 1] - b * u[k]) * r
            for k in range(6, 0, -2):
                for i in range(k):
                    m, m1 = four[i // 2][1][k + 8 * h][i % 2], four[i // 2][1][k + 1 + 8 * h][i % 2]
                    q[i] = q[i] - (m * q[k] + m1 * q[k + 1])
            for i in range(t + h + 1, n):
                if h == 1:
                    cs[i] = [lane_spread(T[i], l + k) for k in range(8)]
                p = [cs[i][k] * q[k] for k in range(8)]
                T[i] = jnp.where(inside, 0.0, T[i]) - (
                    ((p[0] + p[1]) + (p[2] + p[3])) + ((p[4] + p[5]) + (p[6] + p[7])))
    return jnp.concatenate(out, axis=0)


def inverse_factor(D):
    H = B // 2
    lane = lax.broadcasted_iota(jnp.int32, (H, B), 1)
    row = lax.broadcasted_iota(jnp.int32, (H, B), 0)
    top = reduce_half([D[8 * i:8 * i + 8, :] for i in range(H // 8)], 0)
    top = jnp.where((lane >= H) | (lane <= row), top, 0.0)
    low = jnp.where(lane < H, 0.0, D[H:, :]) - mm(top[:, H:], top, 0, 0)
    low = reduce_half([low[8 * i:8 * i + 8, :] for i in range(H // 8)], H)
    return jnp.concatenate(
        [jnp.where(lane < H, top, 0.0), jnp.where(lane <= row + H, low, 0.0)], axis=0)


def add_diag(square, row):
    r = lax.broadcasted_iota(jnp.int32, square.shape, 0)
    c = lax.broadcasted_iota(jnp.int32, square.shape, 1)
    return square + jnp.where(r == c, row, 0.0)


def as_columns(row):
    return jnp.concatenate(
        [jnp.broadcast_to(row[0:1, B * k:B * k + B], (B, B)).T for k in range(NB)], axis=0
    )


def as_row(columns):
    return jnp.concatenate([columns[B * k:B * k + B, :].T[0:8, :] for k in range(NB)], axis=1)


def tree_kernel(
    sizes, rows_ref, leaf_prior_ref, node_rows_ref, node_res_ref, node_prior_ref,
    interior_ref, own_ref,
    t_ref, inv_ref, base_ref, g2_ref, s_ref, c_ref, in_s, in_c, step_ref, u_ref, f_ref,
    shift_ref, gain_ref, land_ref, j1_ref, leaf_send, leaf_recv, up_send, up_recv, down_send, down_recv,
    early_send, early_recv,
):
    grp_count, sub_count = sizes
    count = grp_count * sub_count
    depth = count.bit_length() - 1
    pos = lax.axis_index("grp") * sub_count + lax.axis_index("sub")
    odd = pos % 2 == 1
    even = pos % 2 == 0
    middle = count // 2 - 1
    top = pos == count - 1
    root = pos == middle
    below_root = pos != middle
    odd_node = odd & (pos != count - 1)
    below_top = pos != count - 1
    stride = jnp.int32(0)
    left = jnp.int32(0)
    for level in range(1, depth + 2):
        here = jnp.where((pos + 1) % 2**level == 2 ** (level - 1), 1, 0)
        stride = stride + here * 2 ** (level - 1)
        left = left + here * (1 - (pos + 1) // 2**level % 2)
    parent = jnp.where(top, middle, pos + (2 * left - 1) * stride)
    parent = jnp.where(root, count - 1, parent)
    to_slot = jnp.where(top, 2, 1 - left)
    half = stride // 2

    def device(target):
        return (target // sub_count, target % sub_count)

    def up_copy(phase, n, target, slot):
        if n == NB:
            src, dst = c_ref.at[phase], in_c.at[slot]
        else:
            at = (pl.ds(B * n, B), pl.ds(B * n, W - B * n))
            if n == 0:
                at = (pl.ds(0, B), pl.ds(0, B))
            if n == NB + 1:
                at = (pl.ds(0, B), pl.ds(B, W - B))
            src, dst = s_ref.at[phase, at[0], at[1]], in_s.at[slot, at[0], at[1]]
        return pltpu.make_async_remote_copy(
            src_ref=src, dst_ref=dst, send_sem=up_send.at[phase, n],
            recv_sem=up_recv.at[slot, n], device_id=device(target), device_id_type=MESH)

    def down_copy(dst, n, r, target):
        return pltpu.make_async_remote_copy(
            src_ref=step_ref, dst_ref=dst, send_sem=down_send.at[n], recv_sem=down_recv.at[r],
            device_id=device(target), device_id_type=MESH)

    def early_copy(n):
        src = (base_ref.at[1], t_ref.at[1, :, pl.ds(W, W)], g2_ref.at[1])[n]
        dst = (in_s.at[0], in_s.at[2], in_c.at[0])[n]
        return pltpu.make_async_remote_copy(
            src_ref=src, dst_ref=dst, send_sem=early_send.at[n], recv_sem=early_recv.at[n],
            device_id=device(jnp.where(root, count - 1, middle)), device_id_type=MESH)

    some_other = jnp.where(odd, pos - 1, pos + 1)

    def rows_of(k):
        return slice(B * k, B * k + B)

    group = lax.axis_index("grp")
    place = lax.axis_index("sub")
    slot_rows = rows_ref.shape[1]
    per_block = B // slot_rows

    def leaf_copy(j):
        peer = place
        for bit in range(sub_count.bit_length() - 1):
            if j >> bit & 1:
                peer = peer + 2**bit * (1 - 2 * (place // 2**bit % 2))
        return pltpu.make_async_remote_copy(
            src_ref=rows_ref.at[peer], dst_ref=land_ref.at[j], send_sem=leaf_send.at[j],
            recv_sem=leaf_recv.at[j], device_id=(group, peer), device_id_type=MESH)

    for j in range(1, sub_count):
        leaf_copy(j).start()

    def arrive(k):
        rows = rows_of(k)
        parts = []
        for j in range(per_block * k, per_block * k + per_block):
            if j == 0:
                parts.append(rows_ref[place].astype(jnp.float32))
            else:
                leaf_copy(j).wait_recv()
                parts.append(land_ref[j].astype(jnp.float32))
        block = jnp.concatenate(parts, axis=0)
        t_ref[0, rows, W:] = block[:, NI:]
        line = block[:, :NI]
        j1_ref[rows, :] = line.astype(jnp.bfloat16)
        above = j1_ref[:B * k + B, :]
        scaled = thirds(line * (1.0 / leaf_prior_ref[0:1, :NI]))
        square = mm16(above, scaled[2], 1, 1) + mm16(above, scaled[1], 1, 1)
        square = square + mm16(above, scaled[0], 1, 1)
        for i in range(k):
            part = square[rows_of(i), :]
            if i > 0:
                part = part - mm(t_ref[0, :B * i, rows_of(i)], t_ref[0, :B * i, rows], 0, 0)
            if i < k - 1:
                part = mm(inv_ref[0, rows_of(i), :], part, 1, 0)
            t_ref[0, rows_of(i), rows] = part
        corner = add_diag(square[rows, :], jnp.float32(1.0))
        if k > 1:
            corner = corner - mm(t_ref[0, :B * k - B, rows], t_ref[0, :B * k - B, rows], 0, 0)
        t_ref[0, rows, rows] = corner

    r1 = node_rows_ref[:, :W]
    r2 = node_rows_ref[:, W:]
    res = jnp.broadcast_to(node_res_ref[0:1, :], (16, node_res_ref.shape[1]))
    t_ref[1, :, :W] = add_diag(mm16(r1, r1, 0, 0), node_prior_ref[0:1, :W])

    @pl.when(root)
    def _():
        t_ref[1, :, W:2 * W] = mm16(r2, r1, 0, 0)

    @pl.when(below_root)
    def _():
        t_ref[1, :, W:2 * W] = mm16(r1, r2, 0, 0)

    base_ref[1] = jnp.where(top, 0.0, add_diag(mm16(r2, r2, 0, 0), node_prior_ref[0:1, W:]))
    step_ref[...] = mm16(res, r1, 1, 0)[0:8, :]
    g2_ref[1] = jnp.where(top, 0.0, mm16(res, r2, 1, 0)[0:8, :])

    @pl.when(root)
    def _():
        for n in range(3):
            early_copy(n).start()

    t_ref[0, :, :W] = jnp.zeros((W, W), jnp.float32)
    base_ref[0] = add_diag(jnp.zeros((W, W), jnp.float32), leaf_prior_ref[0:1, NI:])
    g2_ref[0] = jnp.zeros((8, W), jnp.float32)

    def back(phase, first):
        for k in range(NB - 1, -1, -1):
            right = t_ref[phase, rows_of(k), first:]
            if k < NB - 1:
                right = right - mm(
                    t_ref[phase, rows_of(k), B * k + B:W], t_ref[phase, B * k + B:W, first:], 1, 0
                )
            t_ref[phase, rows_of(k), first:] = mm(inv_ref[phase, rows_of(k), :], right, 0, 0)
        shift_ref[phase] = as_row(t_ref[phase, :, 2 * W:])
        if first < 2 * W:
            for n, part in enumerate(thirds(t_ref[phase, :, W:2 * W])):
                gain_ref[phase, n] = part

    def stacked(row):
        return jnp.concatenate([x for x in thirds(jnp.concatenate([row, row], axis=0))], axis=0)

    def unstacked(total):
        return total[32:40] + total[16:24] + total[0:8]

    def less_gain(phase, row):
        stack = stacked(row)
        total = mm16(stack, gain_ref[phase, 2], 1, 1) + mm16(stack, gain_ref[phase, 1], 1, 1)
        total = total + mm16(stack, gain_ref[phase, 0], 1, 1)
        return shift_ref[phase] - unstacked(total)

    def receive(k):
        if k == 0:

            @pl.when(odd)
            def _():
                back(0, W)

            @pl.when(root)
            def _():
                for n in range(3):
                    early_copy(n).wait_send()

            @pl.when(top)
            def _():
                for n in range(3):
                    early_copy(n).wait_recv()
                step_ref[...] += in_c[0]
                t_ref[1, :, :W] += in_s[0]
                t_ref[1, :, W:2 * W] = in_s[2]

        if k == 1:

            @pl.when(odd_node)
            def _():
                up_copy(0, NB, some_other, 0).wait_recv()
                step_ref[...] += in_c[0]

            @pl.when(even)
            def _():
                step_ref[...] += c_ref[0]

            @pl.when(below_top)
            def _():
                up_copy(0, NB, some_other, 1).wait_recv()
                step_ref[...] += in_c[1]

            @pl.when(root)
            def _():
                up_copy(0, NB, some_other, 2).wait_recv()
                step_ref[...] += in_c[2]

            t_ref[1, :, 2 * W:] = as_columns(step_ref[...])

        pieces = [(k, rows_of(k), slice(B * k, B if k == 0 else W))]
        if k == 1:
            pieces = [(NB + 1, rows_of(0), slice(B, W))] + pieces

        for n, rows, cols in pieces:

            @pl.when(odd_node)
            def _():
                up_copy(0, n, some_other, 0).wait_recv()
                t_ref[1, rows, cols] += in_s[0, rows, cols]

            @pl.when(even)
            def _():
                t_ref[1, rows, cols] += s_ref[0, rows, cols]

            @pl.when(below_top)
            def _():
                up_copy(0, n, some_other, 1).wait_recv()
                t_ref[1, rows, cols] += in_s[1, rows, cols]

            @pl.when(root)
            def _():
                up_copy(0, n, some_other, 2).wait_recv()
                t_ref[1, rows, cols] += in_s[2, rows, cols]

    def eliminate(phase, _):
        sign = jnp.where(phase == 0, 1.0, -1.0).astype(jnp.float32)
        for k in range(NB):
            rows = rows_of(k)
            pl.when(phase == 0)(lambda: arrive(k))
            pl.when(phase == 1)(lambda: receive(k))
            block = t_ref[phase, rows, rows]
            if k > 0:
                before = rows_of(k - 1)
                inv = inv_ref[phase, before, :]
                near = mm(inv, t_ref[phase, before, rows], 1, 0)
                t_ref[phase, before, rows] = near
                block = block - mm(near, near, 0, 0)
                col = t_ref[phase, :B * k, rows]
                far = slice(B * k + B, W + QC)
                t_ref[phase, before, far] = mm(inv, t_ref[phase, before, far], 1, 0)
                t_ref[phase, rows, far] -= mm(col, t_ref[phase, :B * k, far], 0, 0)
                if k < NB - 1:
                    after = rows_of(k + 1)
                    ahead = t_ref[phase, :B * k, after]
                    t_ref[phase, after, after] -= mm(ahead, ahead, 0, 0)
            if k >= 2:
                for n in range(NB):
                    y = t_ref[phase, (0 if k == 2 else 2 * B):B * k, W:2 * W]
                    base_ref[phase, rows_of(n), B * n:] += sign * mm(
                        y[:, rows_of(n)], y[:, B * n:], 0, 0
                    )
            inv_ref[phase, rows, :] = inverse_factor(block)
        rows = rows_of(NB - 1)

        target = jnp.where(phase == 0, some_other, parent)
        slot = jnp.where(phase == 0, 1, to_slot)
        sends = jnp.where(phase == 0, odd, below_root)

        def finish(n, cols):
            y = t_ref[phase, rows, W:2 * W]
            r = rows_of(n % (NB + 1))
            s_ref[phase, r, cols] = base_ref[phase, r, cols] + sign * mm(y[:, r], y[:, cols], 0, 0)

        def push(n):
            @pl.when(sends)
            def _():
                up_copy(phase, n, target, slot).start()

        inv = inv_ref[phase, rows, :]
        first = mm(inv, t_ref[phase, rows, W:W + B], 1, 0)
        t_ref[phase, rows, W:W + B] = first
        s_ref[phase, :B, :B] = base_ref[phase, :B, :B] + sign * mm(first, first, 0, 0)
        push(0)
        t_ref[phase, rows, W + B:] = mm(inv, t_ref[phase, rows, W + B:], 1, 0)
        finish(NB + 1, slice(B, W))
        push(NB + 1)
        c_ref[phase] = g2_ref[phase] + sign * mm(
            t_ref[phase, :, 2 * W:2 * W + 8], t_ref[phase, :, W:2 * W], 0, 0
        )
        push(NB)
        for n in range(1, NB):
            finish(n, slice(B * n, W))
            push(n)

        return 0

    lax.fori_loop(0, 2, eliminate, 0)

    @pl.when(below_root)
    def _():
        back(1, W)

        @pl.when(even)
        def _():
            back(0, W)

        down_copy(u_ref, 0, 0, parent).wait_recv()
        step_ref[...] = less_gain(1, u_ref[...])

    @pl.when(root)
    def _():
        back(1, 2 * W)
        step_ref[...] = shift_ref[1]
        down_copy(u_ref, 3, 0, count - 1).start()

    @pl.when(odd_node)
    def _():
        down_copy(u_ref, 0, 0, pos - half).start()
        down_copy(u_ref, 1, 0, pos + half).start()

    @pl.when(odd)
    def _():
        down_copy(f_ref, 2, 1, some_other).wait_recv()

    @pl.when(even)
    def _():
        down_copy(f_ref, 2, 1, some_other).start()
        f_ref[...] = step_ref[...]

    own_ref[...] = step_ref[0:1, :]
    line = unstacked(mm16(stacked(less_gain(0, f_ref[...])), j1_ref[...], 1, 0))
    interior_ref[...] = line[0:1, :] / leaf_prior_ref[0:1, :NI]

    for j in range(1, sub_count):
        leaf_copy(j).wait_send()

    @pl.when(odd)
    def _():
        for n in range(NB + 2):
            up_copy(0, n, some_other, 1).wait_send()

    @pl.when(odd_node)
    def _():
        down_copy(u_ref, 0, 0, pos - half).wait_send()
        down_copy(u_ref, 1, 0, pos + half).wait_send()

    @pl.when(root)
    def _():
        down_copy(u_ref, 3, 0, count - 1).wait_send()

    @pl.when(even)
    def _():
        down_copy(f_ref, 2, 1, some_other).wait_send()

    @pl.when(below_root)
    def _():
        for n in range(NB + 2):
            up_copy(1, n, parent, to_slot).wait_send()


def shards(
    sizes,
    measurement_block_rows,
    measurement_residual,
    owner,
    submap_prior_weight,
    separator_measure_rows,
    separator_residual,
    separator_prior_weight,
):
    sub_count = sizes[1]
    block_list, rows_per_block, column_count = measurement_block_rows.shape
    capacity = 2 * block_list // sub_count
    owners = owner[:, 0]
    onehot_own = (owners[:, None] == jnp.arange(sub_count, dtype=jnp.int32)[None, :]).astype(
        jnp.int32
    )
    earlier = jnp.cumsum(onehot_own, axis=0) - onehot_own
    slot_rank = jnp.sum(earlier * onehot_own, axis=1)
    slot_of = owners * capacity + slot_rank
    placement_table = (
        jnp.arange(sub_count * capacity, dtype=jnp.int32)[:, None] == slot_of[None, :]
    ).astype(jnp.bfloat16)
    wide = column_count + B
    full_rows = jnp.concatenate(
        [
            measurement_block_rows,
            jnp.broadcast_to(
                measurement_residual[:, :, None], (block_list, rows_per_block, B)
            ),
        ],
        axis=2,
    ).reshape(block_list, rows_per_block * wide)
    sent_rows = jnp.dot(placement_table, full_rows, preferred_element_type=jnp.bfloat16)
    sent_rows = sent_rows.reshape(sub_count, capacity * rows_per_block, wide)
    vmem = pl.BlockSpec(memory_space=pltpu.VMEM)
    f32 = jnp.float32
    interior, own = pl.pallas_call(
        lambda *refs: tree_kernel(sizes, *refs),
        out_shape=(
            jax.ShapeDtypeStruct((1, NI), f32),
            jax.ShapeDtypeStruct((1, W), f32),
        ),
        in_specs=[vmem] * 5,
        out_specs=(vmem, vmem),
        scratch_shapes=[
            pltpu.VMEM((2, W, W + QC), f32),
            pltpu.VMEM((2, W, B), f32),
            pltpu.VMEM((2, W, W), f32),
            pltpu.VMEM((2, 8, W), f32),
            pltpu.VMEM((2, W, W), f32),
            pltpu.VMEM((2, 8, W), f32),
            pltpu.VMEM((3, W, W), f32),
            pltpu.VMEM((3, 8, W), f32),
            pltpu.VMEM((8, W), f32),
            pltpu.VMEM((8, W), f32),
            pltpu.VMEM((8, W), f32),
            pltpu.VMEM((2, 8, W), f32),
            pltpu.VMEM((2, 3, W, W), jnp.bfloat16),
            pltpu.VMEM(sent_rows.shape, jnp.bfloat16),
            pltpu.VMEM((W, NI), jnp.bfloat16),
            pltpu.SemaphoreType.DMA((sub_count,)),
            pltpu.SemaphoreType.DMA((sub_count,)),
            pltpu.SemaphoreType.DMA((2, NB + 2)),
            pltpu.SemaphoreType.DMA((3, NB + 2)),
            pltpu.SemaphoreType.DMA((4,)),
            pltpu.SemaphoreType.DMA((2,)),
            pltpu.SemaphoreType.DMA((3,)),
            pltpu.SemaphoreType.DMA((3,)),
        ],
        compiler_params=pltpu.CompilerParams(
            has_side_effects=True, vmem_limit_bytes=56 * 2**20
        ),
    )(
        sent_rows,
        submap_prior_weight,
        separator_measure_rows,
        separator_residual,
        separator_prior_weight,
    )
    return (interior, own)


def solution(mesh):
    sizes = (mesh.shape["grp"], mesh.shape["sub"])
    return jax.shard_map(
        lambda *args: shards(sizes, *args),
        mesh=mesh,
        in_specs=(
            P(("grp", "sub"), None, None),
            P(("grp", "sub"), None),
            P(("grp", "sub"), None),
            P(("grp", "sub"), None),
            P(("grp", "sub"), None),
            P(("grp", "sub"), None),
            P(("grp", "sub"), None),
        ),
        out_specs=(P(("grp", "sub"), None), P(("grp", "sub"), None)),
        check_vma=False,
    )
```

```python
import jax
import jax.numpy as jnp
from jax import lax
from jax.experimental import pallas as pl
from jax.experimental.pallas import tpu as pltpu
from jax.sharding import PartitionSpec as P

NI = 1024
W = 512
B = 128
NB = W // B
QC = W + B
MESH = pl.DeviceIdType.MESH
highest = lax.Precision.HIGHEST


def mm(a, b, ca, cb):
    return lax.dot_general(
        a, b, (((ca,), (cb,)), ((), ())), precision=highest, preferred_element_type=jnp.float32
    )


def mm16(a, b, ca, cb):
    return lax.dot_general(a, b, (((ca,), (cb,)), ((), ())), preferred_element_type=jnp.float32)


def thirds(x):
    hi = x.astype(jnp.bfloat16)
    rest = x - hi.astype(jnp.float32)
    mid = rest.astype(jnp.bfloat16)
    low = (rest - mid.astype(jnp.float32)).astype(jnp.bfloat16)
    return hi, mid, low


def lane_spread(v, j):
    return jnp.broadcast_to(v[:, j:j + 1], (8, B))


def row_spread(v, i):
    return jnp.broadcast_to(v[i:i + 1, :], (8, B))


def pivot_pair(C, k):
    h, i = k // 8, k % 8
    X, Y = C[h][k], C[h][k + 1]
    a, b, c = row_spread(X, i), row_spread(X, i + 1), row_spread(Y, i + 1)
    r = 1.0 / (a * c - b * b)
    N, M = {}, {}
    for g in range(h, 2):
        Xg, Yg = C[g][k], C[g][k + 1]
        N[g] = (Xg * c - Yg * b, Yg * a - Xg * b)
        M[g] = (N[g][0] * r, N[g][1] * r)
    m = {}
    for j in range(k + 2, 16):
        hj = j // 8
        m[j] = (row_spread(M[hj][0], j % 8), row_spread(M[hj][1], j % 8))
        if j < k + 4:
            x, y = row_spread(C[hj][k], j % 8), row_spread(C[hj][k + 1], j % 8)
            for g in range(hj, 2):
                C[g][j] = C[g][j] - r * (N[g][0] * x + N[g][1] * y)
        else:
            for g in range(hj, 2):
                C[g][j] = C[g][j] - (C[g][k] * m[j][0] + C[g][k + 1] * m[j][1])
    return (a, b, c, r), m


def scaled_rows(u, pairs, sub):
    def join(parts, step):
        total = parts[0]
        for n in range(1, len(parts)):
            total = jnp.where(sub >= n * step, parts[n], total)
        return total

    a, b, r = (join([p[0][n] for p in pairs], 2) for n in (0, 1, 3))
    U, V = join(u, 1), join(u[0::2], 2)
    ra = lax.rsqrt(a)
    d = a * r
    return jnp.where(sub % 2 == 1, (U - (b * (ra * ra)) * V) * (d * lax.rsqrt(d)), U * ra)


def reduce_half(T, off):
    lane = lax.broadcasted_iota(jnp.int32, (8, B), 1)
    sub = lax.broadcasted_iota(jnp.int32, (8, B), 0)
    T = list(T)
    out = []
    n = len(T)
    for t in range(0, n, 2):
        la = off + 8 * t
        C = [[lane_spread(T[t], la + k) for k in range(8)],
             [lane_spread(T[t + 1], la + k) for k in range(16)]]
        cs = {i: [lane_spread(T[i], la + k) for k in range(8)] for i in range(t + 2, n)}
        cs[t + 1] = C[1][:8]
        pairs = [pivot_pair(C, k) for k in range(0, 16, 2)]
        for h in range(2):
            l = la + 8 * h
            inside = (lane >= l) & (lane < l + 8)
            base = jnp.where(inside, jnp.where(lane == sub + l, 1.0, 0.0), T[t + h])
            u = [row_spread(base, k) for k in range(8)]
            four = pairs[4 * h:4 * h + 4]
            for k in range(0, 6, 2):
                for i in range(k + 2, 8):
                    m = four[k // 2][1][i + 8 * h]
                    u[i] = u[i] - (m[0] * u[k] + m[1] * u[k + 1])
            out.append(scaled_rows(u, four, sub))
            if t + h + 1 == n:
                break
            q = [None] * 8
            for k in range(6, -1, -2):
                a, b, c, r = four[k // 2][0]
                q[k] = (c * u[k] - b * u[k + 1]) * r
                q[k + 1] = (a * u[k + 1] - b * u[k]) * r
            for k in range(6, 0, -2):
                for i in range(k):
                    m, m1 = four[i // 2][1][k + 8 * h][i % 2], four[i // 2][1][k + 1 + 8 * h][i % 2]
                    q[i] = q[i] - (m * q[k] + m1 * q[k + 1])
            for i in range(t + h + 1, n):
                if h == 1:
                    cs[i] = [lane_spread(T[i], l + k) for k in range(8)]
                p = [cs[i][k] * q[k] for k in range(8)]
                T[i] = jnp.where(inside, 0.0, T[i]) - (
                    ((p[0] + p[1]) + (p[2] + p[3])) + ((p[4] + p[5]) + (p[6] + p[7])))
    return jnp.concatenate(out, axis=0)


def inverse_factor(D):
    H = B // 2
    lane = lax.broadcasted_iota(jnp.int32, (H, B), 1)
    row = lax.broadcasted_iota(jnp.int32, (H, B), 0)
    top = reduce_half([D[8 * i:8 * i + 8, :] for i in range(H // 8)], 0)
    top = jnp.where((lane >= H) | (lane <= row), top, 0.0)
    low = jnp.where(lane < H, 0.0, D[H:, :]) - mm(top[:, H:], top, 0, 0)
    low = reduce_half([low[8 * i:8 * i + 8, :] for i in range(H // 8)], H)
    return jnp.concatenate(
        [jnp.where(lane < H, top, 0.0), jnp.where(lane <= row + H, low, 0.0)], axis=0)


def add_diag(square, row):
    r = lax.broadcasted_iota(jnp.int32, square.shape, 0)
    c = lax.broadcasted_iota(jnp.int32, square.shape, 1)
    return square + jnp.where(r == c, row, 0.0)


def as_columns(row):
    return jnp.concatenate(
        [jnp.broadcast_to(row[0:1, B * k:B * k + B], (B, B)).T for k in range(NB)], axis=0
    )


def as_row(columns):
    return jnp.concatenate([columns[B * k:B * k + B, :].T[0:8, :] for k in range(NB)], axis=1)


def tree_kernel(
    sizes, blocks_ref, block_res_ref, owner_ref, leaf_prior_ref, node_rows_ref, node_res_ref, node_prior_ref,
    interior_ref, own_ref,
    t_ref, inv_ref, base_ref, g2_ref, s_ref, c_ref, in_s, in_c, step_ref, u_ref, f_ref,
    shift_ref, gain_ref, land_ref, j1_ref, leaf_send, leaf_recv, up_send, up_recv, down_send, down_recv,
    early_send, early_recv, rows_ref, res_ref, land_res_ref, res_send, res_recv,
):
    grp_count, sub_count = sizes
    count = grp_count * sub_count
    depth = count.bit_length() - 1
    pos = lax.axis_index("grp") * sub_count + lax.axis_index("sub")
    odd = pos % 2 == 1
    even = pos % 2 == 0
    middle = count // 2 - 1
    top = pos == count - 1
    root = pos == middle
    below_root = pos != middle
    odd_node = odd & (pos != count - 1)
    below_top = pos != count - 1
    stride = jnp.int32(0)
    left = jnp.int32(0)
    for level in range(1, depth + 2):
        here = jnp.where((pos + 1) % 2**level == 2 ** (level - 1), 1, 0)
        stride = stride + here * 2 ** (level - 1)
        left = left + here * (1 - (pos + 1) // 2**level % 2)
    parent = jnp.where(top, middle, pos + (2 * left - 1) * stride)
    parent = jnp.where(root, count - 1, parent)
    to_slot = jnp.where(top, 2, 1 - left)
    half = stride // 2

    def device(target):
        return (target // sub_count, target % sub_count)

    def up_copy(phase, n, target, slot):
        if n == NB:
            src, dst = c_ref.at[phase], in_c.at[slot]
        else:
            at = (pl.ds(B * n, B), pl.ds(B * n, W - B * n))
            if n == 0:
                at = (pl.ds(0, B), pl.ds(0, B))
            if n == NB + 1:
                at = (pl.ds(0, B), pl.ds(B, W - B))
            src, dst = s_ref.at[phase, at[0], at[1]], in_s.at[slot, at[0], at[1]]
        return pltpu.make_async_remote_copy(
            src_ref=src, dst_ref=dst, send_sem=up_send.at[phase, n],
            recv_sem=up_recv.at[slot, n], device_id=device(target), device_id_type=MESH)

    def down_copy(dst, n, r, target):
        return pltpu.make_async_remote_copy(
            src_ref=step_ref, dst_ref=dst, send_sem=down_send.at[n], recv_sem=down_recv.at[r],
            device_id=device(target), device_id_type=MESH)

    def early_copy(n):
        src = (base_ref.at[1], t_ref.at[1, :, pl.ds(W, W)], g2_ref.at[1])[n]
        dst = (in_s.at[0], in_s.at[2], in_c.at[0])[n]
        return pltpu.make_async_remote_copy(
            src_ref=src, dst_ref=dst, send_sem=early_send.at[n], recv_sem=early_recv.at[n],
            device_id=device(jnp.where(root, count - 1, middle)), device_id_type=MESH)

    some_other = jnp.where(odd, pos - 1, pos + 1)

    def rows_of(k):
        return slice(B * k, B * k + B)

    group = lax.axis_index("grp")
    place = lax.axis_index("sub")
    slot_rows = 2 * blocks_ref.shape[0] // sub_count * blocks_ref.shape[1]
    per_block = B // slot_rows

    def peer_of(j):
        peer = place
        for bit in range(sub_count.bit_length() - 1):
            if j >> bit & 1:
                peer = peer + 2**bit * (1 - 2 * (place // 2**bit % 2))
        return peer

    def leaf_copy(j):
        peer = peer_of(j)
        return pltpu.make_async_remote_copy(
            src_ref=rows_ref.at[peer], dst_ref=land_ref.at[j], send_sem=leaf_send.at[j],
            recv_sem=leaf_recv.at[j], device_id=(group, peer), device_id_type=MESH)

    def res_copy(j):
        return pltpu.make_async_remote_copy(
            src_ref=res_ref.at[j], dst_ref=land_res_ref.at[j], send_sem=res_send.at[j],
            recv_sem=res_recv.at[j], device_id=(group, peer_of(j)), device_id_type=MESH)

    block_list, per, columns = blocks_ref.shape
    held = block_list * per
    f32, bf16 = jnp.float32, jnp.bfloat16

    def grid(shape, dim):
        return lax.broadcasted_iota(jnp.int32, shape, dim)

    def many(row):
        return jnp.broadcast_to(row, (16, row.shape[1])).astype(bf16)

    repeat = jnp.where(
        grid((block_list, held), 1) // per == grid((block_list, held), 0), 1.0, 0.0
    ).astype(bf16)
    earlier = jnp.where(
        grid((block_list, block_list), 0) < grid((block_list, block_list), 1), 1.0, 0.0
    ).astype(bf16)
    kinds = max(sub_count, 16)
    names = jnp.where(grid((kinds, block_list), 0) == owner_ref[0:1, :], 1.0, 0.0)
    ahead_of = jnp.sum(mm16(names.astype(bf16), earlier, 1, 0) * names, axis=0, keepdims=True)
    rank = mm16(many(ahead_of), repeat, 1, 0)[0:1, :]
    named = mm16(many(owner_ref[0:1, :].astype(f32)), repeat, 1, 0)[0:1, :]
    at_row = (rank * per).astype(jnp.int32) + grid((1, held), 1) % per
    named = named.astype(jnp.int32)
    table = jnp.where(
        grid((sub_count * slot_rows, held), 0) == named * slot_rows + at_row, 1.0, 0.0
    ).astype(bf16)
    placed = mm16(table, blocks_ref[...].reshape(held, columns), 1, 0)
    for n in range(sub_count):
        rows_ref[n] = placed[slot_rows * n:slot_rows * (n + 1), :].astype(bf16)
    for j in range(1, sub_count):
        leaf_copy(j).start()
    spread = mm16(
        jnp.concatenate([block_res_ref[...].astype(f32), jnp.zeros((16 - per, block_list), f32)], axis=0).astype(bf16),
        repeat, 1, 0,
    )
    spread = jnp.where(grid((16, held), 0) == grid((16, held), 1) % per, spread, 0.0)
    line_res = many(jnp.sum(spread, axis=0, keepdims=True))
    for j in range(sub_count):
        hit = grid((B, held), 0) == at_row + (j % per_block) * slot_rows
        hit = jnp.where(hit & (named == peer_of(j)), 1.0, 0.0).astype(bf16)
        res_ref[j] = mm16(line_res, hit, 1, 1).astype(bf16)
        if j > 0:
            res_copy(j).start()

    def arrive(k):
        rows = rows_of(k)
        parts = []
        values = jnp.zeros((16, B), f32)
        for j in range(per_block * k, per_block * k + per_block):
            if j == 0:
                parts.append(rows_ref[place].astype(f32))
                values = values + res_ref[0].astype(f32)
            else:
                leaf_copy(j).wait_recv()
                res_copy(j).wait_recv()
                parts.append(land_ref[j].astype(f32))
                values = values + land_res_ref[j].astype(f32)
        block = jnp.concatenate(parts, axis=0)
        t_ref[0, rows, W:2 * W] = block[:, NI:]
        t_ref[0, rows, 2 * W:] = jnp.broadcast_to(values[0:1, :], (B, B)).T
        line = block[:, :NI]
        j1_ref[rows, :] = line.astype(jnp.bfloat16)
        above = j1_ref[:B * k + B, :]
        scaled = thirds(line * (1.0 / leaf_prior_ref[0:1, :NI]))
        square = mm16(above, scaled[2], 1, 1) + mm16(above, scaled[1], 1, 1)
        square = square + mm16(above, scaled[0], 1, 1)
        for i in range(k):
            part = square[rows_of(i), :]
            if i > 0:
                part = part - mm(t_ref[0, :B * i, rows_of(i)], t_ref[0, :B * i, rows], 0, 0)
            if i < k - 1:
                part = mm(inv_ref[0, rows_of(i), :], part, 1, 0)
            t_ref[0, rows_of(i), rows] = part
        corner = add_diag(square[rows, :], jnp.float32(1.0))
        if k > 1:
            corner = corner - mm(t_ref[0, :B * k - B, rows], t_ref[0, :B * k - B, rows], 0, 0)
        t_ref[0, rows, rows] = corner

    r1 = node_rows_ref[:, :W]
    r2 = node_rows_ref[:, W:]
    res = jnp.broadcast_to(node_res_ref[0:1, :], (16, node_res_ref.shape[1]))
    t_ref[1, :, :W] = add_diag(mm16(r1, r1, 0, 0), node_prior_ref[0:1, :W])

    @pl.when(root)
    def _():
        t_ref[1, :, W:2 * W] = mm16(r2, r1, 0, 0)

    @pl.when(below_root)
    def _():
        t_ref[1, :, W:2 * W] = mm16(r1, r2, 0, 0)

    base_ref[1] = jnp.where(top, 0.0, add_diag(mm16(r2, r2, 0, 0), node_prior_ref[0:1, W:]))
    step_ref[...] = mm16(res, r1, 1, 0)[0:8, :]
    g2_ref[1] = jnp.where(top, 0.0, mm16(res, r2, 1, 0)[0:8, :])

    @pl.when(root)
    def _():
        for n in range(3):
            early_copy(n).start()

    t_ref[0, :, :W] = jnp.zeros((W, W), jnp.float32)
    base_ref[0] = add_diag(jnp.zeros((W, W), jnp.float32), leaf_prior_ref[0:1, NI:])
    g2_ref[0] = jnp.zeros((8, W), jnp.float32)

    def back(phase, first):
        for k in range(NB - 1, -1, -1):
            right = t_ref[phase, rows_of(k), first:]
            if k < NB - 1:
                right = right - mm(
                    t_ref[phase, rows_of(k), B * k + B:W], t_ref[phase, B * k + B:W, first:], 1, 0
                )
            t_ref[phase, rows_of(k), first:] = mm(inv_ref[phase, rows_of(k), :], right, 0, 0)
        shift_ref[phase] = as_row(t_ref[phase, :, 2 * W:])
        if first < 2 * W:
            for n, part in enumerate(thirds(t_ref[phase, :, W:2 * W])):
                gain_ref[phase, n] = part

    def stacked(row):
        return jnp.concatenate([x for x in thirds(jnp.concatenate([row, row], axis=0))], axis=0)

    def unstacked(total):
        return total[32:40] + total[16:24] + total[0:8]

    def less_gain(phase, row):
        stack = stacked(row)
        total = mm16(stack, gain_ref[phase, 2], 1, 1) + mm16(stack, gain_ref[phase, 1], 1, 1)
        total = total + mm16(stack, gain_ref[phase, 0], 1, 1)
        return shift_ref[phase] - unstacked(total)

    def receive(k):
        if k == 0:

            @pl.when(odd)
            def _():
                back(0, W)

            @pl.when(root)
            def _():
                for n in range(3):
                    early_copy(n).wait_send()

            @pl.when(top)
            def _():
                for n in range(3):
                    early_copy(n).wait_recv()
                step_ref[...] += in_c[0]
                t_ref[1, :, :W] += in_s[0]
                t_ref[1, :, W:2 * W] = in_s[2]

        if k == 1:

            @pl.when(odd_node)
            def _():
                up_copy(0, NB, some_other, 0).wait_recv()
                step_ref[...] += in_c[0]

            @pl.when(even)
            def _():
                step_ref[...] += c_ref[0]

            @pl.when(below_top)
            def _():
                up_copy(0, NB, some_other, 1).wait_recv()
                step_ref[...] += in_c[1]

            @pl.when(root)
            def _():
                up_copy(0, NB, some_other, 2).wait_recv()
                step_ref[...] += in_c[2]

            t_ref[1, :, 2 * W:] = as_columns(step_ref[...])

        pieces = [(k, rows_of(k), slice(B * k, B if k == 0 else W))]
        if k == 1:
            pieces = [(NB + 1, rows_of(0), slice(B, W))] + pieces

        for n, rows, cols in pieces:

            @pl.when(odd_node)
            def _():
                up_copy(0, n, some_other, 0).wait_recv()
                t_ref[1, rows, cols] += in_s[0, rows, cols]

            @pl.when(even)
            def _():
                t_ref[1, rows, cols] += s_ref[0, rows, cols]

            @pl.when(below_top)
            def _():
                up_copy(0, n, some_other, 1).wait_recv()
                t_ref[1, rows, cols] += in_s[1, rows, cols]

            @pl.when(root)
            def _():
                up_copy(0, n, some_other, 2).wait_recv()
                t_ref[1, rows, cols] += in_s[2, rows, cols]

    def eliminate(phase, _):
        sign = jnp.where(phase == 0, 1.0, -1.0).astype(jnp.float32)
        for k in range(NB):
            rows = rows_of(k)
            pl.when(phase == 0)(lambda: arrive(k))
            pl.when(phase == 1)(lambda: receive(k))
            block = t_ref[phase, rows, rows]
            if k > 0:
                before = rows_of(k - 1)
                inv = inv_ref[phase, before, :]
                near = mm(inv, t_ref[phase, before, rows], 1, 0)
                t_ref[phase, before, rows] = near
                block = block - mm(near, near, 0, 0)
                col = t_ref[phase, :B * k, rows]
                far = slice(B * k + B, W + QC)
                t_ref[phase, before, far] = mm(inv, t_ref[phase, before, far], 1, 0)
                t_ref[phase, rows, far] -= mm(col, t_ref[phase, :B * k, far], 0, 0)
                if k < NB - 1:
                    after = rows_of(k + 1)
                    ahead = t_ref[phase, :B * k, after]
                    t_ref[phase, after, after] -= mm(ahead, ahead, 0, 0)
            if k >= 2:
                for n in range(NB):
                    y = t_ref[phase, (0 if k == 2 else 2 * B):B * k, W:2 * W]
                    base_ref[phase, rows_of(n), B * n:] += sign * mm(
                        y[:, rows_of(n)], y[:, B * n:], 0, 0
                    )
            inv_ref[phase, rows, :] = inverse_factor(block)
        rows = rows_of(NB - 1)

        target = jnp.where(phase == 0, some_other, parent)
        slot = jnp.where(phase == 0, 1, to_slot)
        sends = jnp.where(phase == 0, odd, below_root)

        def finish(n, cols):
            y = t_ref[phase, rows, W:2 * W]
            r = rows_of(n % (NB + 1))
            s_ref[phase, r, cols] = base_ref[phase, r, cols] + sign * mm(y[:, r], y[:, cols], 0, 0)

        def push(n):
            @pl.when(sends)
            def _():
                up_copy(phase, n, target, slot).start()

        inv = inv_ref[phase, rows, :]
        first = mm(inv, t_ref[phase, rows, W:W + B], 1, 0)
        t_ref[phase, rows, W:W + B] = first
        s_ref[phase, :B, :B] = base_ref[phase, :B, :B] + sign * mm(first, first, 0, 0)
        push(0)
        t_ref[phase, rows, W + B:] = mm(inv, t_ref[phase, rows, W + B:], 1, 0)
        finish(NB + 1, slice(B, W))
        push(NB + 1)
        c_ref[phase] = g2_ref[phase] + sign * mm(
            t_ref[phase, :, 2 * W:2 * W + 8], t_ref[phase, :, W:2 * W], 0, 0
        )
        push(NB)
        for n in range(1, NB):
            finish(n, slice(B * n, W))
            push(n)

        return 0

    lax.fori_loop(0, 2, eliminate, 0)

    @pl.when(below_root)
    def _():
        back(1, W)

        @pl.when(even)
        def _():
            back(0, W)

        down_copy(u_ref, 0, 0, parent).wait_recv()
        step_ref[...] = less_gain(1, u_ref[...])

    @pl.when(root)
    def _():
        back(1, 2 * W)
        step_ref[...] = shift_ref[1]
        down_copy(u_ref, 3, 0, count - 1).start()

    @pl.when(odd_node)
    def _():
        down_copy(u_ref, 0, 0, pos - half).start()
        down_copy(u_ref, 1, 0, pos + half).start()

    @pl.when(odd)
    def _():
        down_copy(f_ref, 2, 1, some_other).wait_recv()

    @pl.when(even)
    def _():
        down_copy(f_ref, 2, 1, some_other).start()
        f_ref[...] = step_ref[...]

    own_ref[...] = step_ref[0:1, :]
    line = unstacked(mm16(stacked(less_gain(0, f_ref[...])), j1_ref[...], 1, 0))
    interior_ref[...] = line[0:1, :] / leaf_prior_ref[0:1, :NI]

    for j in range(1, sub_count):
        leaf_copy(j).wait_send()
        res_copy(j).wait_send()

    @pl.when(odd)
    def _():
        for n in range(NB + 2):
            up_copy(0, n, some_other, 1).wait_send()

    @pl.when(odd_node)
    def _():
        down_copy(u_ref, 0, 0, pos - half).wait_send()
        down_copy(u_ref, 1, 0, pos + half).wait_send()

    @pl.when(root)
    def _():
        down_copy(u_ref, 3, 0, count - 1).wait_send()

    @pl.when(even)
    def _():
        down_copy(f_ref, 2, 1, some_other).wait_send()

    @pl.when(below_root)
    def _():
        for n in range(NB + 2):
            up_copy(1, n, parent, to_slot).wait_send()


def shards(
    sizes,
    measurement_block_rows,
    measurement_residual,
    owner,
    submap_prior_weight,
    separator_measure_rows,
    separator_residual,
    separator_prior_weight,
):
    sub_count = sizes[1]
    block_list, rows_per_block, column_count = measurement_block_rows.shape
    slot_rows = 2 * block_list // sub_count * rows_per_block
    vmem = pl.BlockSpec(memory_space=pltpu.VMEM)
    f32 = jnp.float32
    interior, own = pl.pallas_call(
        lambda *refs: tree_kernel(sizes, *refs),
        out_shape=(
            jax.ShapeDtypeStruct((1, NI), f32),
            jax.ShapeDtypeStruct((1, W), f32),
        ),
        in_specs=[vmem] * 7,
        out_specs=(vmem, vmem),
        scratch_shapes=[
            pltpu.VMEM((2, W, W + QC), f32),
            pltpu.VMEM((2, W, B), f32),
            pltpu.VMEM((2, W, W), f32),
            pltpu.VMEM((2, 8, W), f32),
            pltpu.VMEM((2, W, W), f32),
            pltpu.VMEM((2, 8, W), f32),
            pltpu.VMEM((3, W, W), f32),
            pltpu.VMEM((3, 8, W), f32),
            pltpu.VMEM((8, W), f32),
            pltpu.VMEM((8, W), f32),
            pltpu.VMEM((8, W), f32),
            pltpu.VMEM((2, 8, W), f32),
            pltpu.VMEM((2, 3, W, W), jnp.bfloat16),
            pltpu.VMEM((sub_count, slot_rows, column_count), jnp.bfloat16),
            pltpu.VMEM((W, NI), jnp.bfloat16),
            pltpu.SemaphoreType.DMA((sub_count,)),
            pltpu.SemaphoreType.DMA((sub_count,)),
            pltpu.SemaphoreType.DMA((2, NB + 2)),
            pltpu.SemaphoreType.DMA((3, NB + 2)),
            pltpu.SemaphoreType.DMA((4,)),
            pltpu.SemaphoreType.DMA((2,)),
            pltpu.SemaphoreType.DMA((3,)),
            pltpu.SemaphoreType.DMA((3,)),
            pltpu.VMEM((sub_count, slot_rows, column_count), jnp.bfloat16),
            pltpu.VMEM((sub_count, 16, B), jnp.bfloat16),
            pltpu.VMEM((sub_count, 16, B), jnp.bfloat16),
            pltpu.SemaphoreType.DMA((sub_count,)),
            pltpu.SemaphoreType.DMA((sub_count,)),
        ],
        compiler_params=pltpu.CompilerParams(
            has_side_effects=True, vmem_limit_bytes=56 * 2**20
        ),
    )(
        measurement_block_rows,
        measurement_residual.T,
        owner.T,
        submap_prior_weight,
        separator_measure_rows,
        separator_residual,
        separator_prior_weight,
    )

    def pass_on(a_ref, b_ref, a_out, b_out):
        a_out[...] = a_ref[...]
        b_out[...] = b_ref[...]

    return tuple(pl.pallas_call(
        pass_on,
        out_shape=(jax.ShapeDtypeStruct((1, NI), f32), jax.ShapeDtypeStruct((1, W), f32)),
        in_specs=[vmem] * 2,
        out_specs=(vmem, vmem),
    )(interior, own))


def solution(mesh):
    sizes = (mesh.shape["grp"], mesh.shape["sub"])
    return jax.shard_map(
        lambda *args: shards(sizes, *args),
        mesh=mesh,
        in_specs=(
            P(("grp", "sub"), None, None),
            P(("grp", "sub"), None),
            P(("grp", "sub"), None),
            P(("grp", "sub"), None),
            P(("grp", "sub"), None),
            P(("grp", "sub"), None),
            P(("grp", "sub"), None),
        ),
        out_specs=(P(("grp", "sub"), None), P(("grp", "sub"), None)),
        check_vma=False,
    )
```

```python
import jax
import jax.numpy as jnp
from jax import lax
from jax.experimental import pallas as pl
from jax.experimental.pallas import tpu as pltpu
from jax.sharding import PartitionSpec as P

NI = 1024
W = 512
B = 128
NB = W // B
MESH = pl.DeviceIdType.MESH
highest = lax.Precision.HIGHEST


def mm(a, b, ca, cb):
    return lax.dot_general(
        a, b, (((ca,), (cb,)), ((), ())), precision=highest, preferred_element_type=jnp.float32
    )


def mm16(a, b, ca, cb):
    return lax.dot_general(a, b, (((ca,), (cb,)), ((), ())), preferred_element_type=jnp.float32)


def thirds(x):
    hi = x.astype(jnp.bfloat16)
    rest = x - hi.astype(jnp.float32)
    mid = rest.astype(jnp.bfloat16)
    low = (rest - mid.astype(jnp.float32)).astype(jnp.bfloat16)
    return hi, mid, low


def lane_spread(v, j):
    return jnp.broadcast_to(v[:, j:j + 1], (8, B))


def row_spread(v, i):
    return jnp.broadcast_to(v[i:i + 1, :], (8, B))


def pivot_pair(C, k):
    h, i = k // 8, k % 8
    X, Y = C[h][k], C[h][k + 1]
    a, b, c = row_spread(X, i), row_spread(X, i + 1), row_spread(Y, i + 1)
    r = 1.0 / (a * c - b * b)
    N, M = {}, {}
    for g in range(h, 2):
        Xg, Yg = C[g][k], C[g][k + 1]
        N[g] = (Xg * c - Yg * b, Yg * a - Xg * b)
        M[g] = (N[g][0] * r, N[g][1] * r)
    m = {}
    for j in range(k + 2, 16):
        hj = j // 8
        m[j] = (row_spread(M[hj][0], j % 8), row_spread(M[hj][1], j % 8))
        if j < k + 4:
            x, y = row_spread(C[hj][k], j % 8), row_spread(C[hj][k + 1], j % 8)
            for g in range(hj, 2):
                C[g][j] = C[g][j] - r * (N[g][0] * x + N[g][1] * y)
        else:
            for g in range(hj, 2):
                C[g][j] = C[g][j] - (C[g][k] * m[j][0] + C[g][k + 1] * m[j][1])
    return (a, b, c, r), m


def scaled_rows(u, pairs, sub):
    def join(parts, step):
        total = parts[0]
        for n in range(1, len(parts)):
            total = jnp.where(sub >= n * step, parts[n], total)
        return total

    a, b, r = (join([p[0][n] for p in pairs], 2) for n in (0, 1, 3))
    U, V = join(u, 1), join(u[0::2], 2)
    ra = lax.rsqrt(a)
    d = a * r
    return jnp.where(sub % 2 == 1, (U - (b * (ra * ra)) * V) * (d * lax.rsqrt(d)), U * ra)


def reduce_half(T, off):
    lane = lax.broadcasted_iota(jnp.int32, (8, B), 1)
    sub = lax.broadcasted_iota(jnp.int32, (8, B), 0)
    T = list(T)
    out = []
    n = len(T)
    for t in range(0, n, 2):
        la = off + 8 * t
        C = [[lane_spread(T[t], la + k) for k in range(8)],
             [lane_spread(T[t + 1], la + k) for k in range(16)]]
        cs = {i: [lane_spread(T[i], la + k) for k in range(8)] for i in range(t + 2, n)}
        cs[t + 1] = C[1][:8]
        pairs = [pivot_pair(C, k) for k in range(0, 16, 2)]
        for h in range(2):
            l = la + 8 * h
            inside = (lane >= l) & (lane < l + 8)
            base = jnp.where(inside, jnp.where(lane == sub + l, 1.0, 0.0), T[t + h])
            u = [row_spread(base, k) for k in range(8)]
            four = pairs[4 * h:4 * h + 4]
            for k in range(0, 6, 2):
                for i in range(k + 2, 8):
                    m = four[k // 2][1][i + 8 * h]
                    u[i] = u[i] - (m[0] * u[k] + m[1] * u[k + 1])
            out.append(scaled_rows(u, four, sub))
            if t + h + 1 == n:
                break
            q = [None] * 8
            for k in range(6, -1, -2):
                a, b, c, r = four[k // 2][0]
                q[k] = (c * u[k] - b * u[k + 1]) * r
                q[k + 1] = (a * u[k + 1] - b * u[k]) * r
            for k in range(6, 0, -2):
                for i in range(k):
                    m, m1 = four[i // 2][1][k + 8 * h][i % 2], four[i // 2][1][k + 1 + 8 * h][i % 2]
                    q[i] = q[i] - (m * q[k] + m1 * q[k + 1])
            for i in range(t + h + 1, n):
                if h == 1:
                    cs[i] = [lane_spread(T[i], l + k) for k in range(8)]
                p = [cs[i][k] * q[k] for k in range(8)]
                T[i] = jnp.where(inside, 0.0, T[i]) - (
                    ((p[0] + p[1]) + (p[2] + p[3])) + ((p[4] + p[5]) + (p[6] + p[7])))
    return jnp.concatenate(out, axis=0)


def inverse_factor(D):
    H = B // 2
    lane = lax.broadcasted_iota(jnp.int32, (H, B), 1)
    row = lax.broadcasted_iota(jnp.int32, (H, B), 0)
    top = reduce_half([D[8 * i:8 * i + 8, :] for i in range(H // 8)], 0)
    top = jnp.where((lane >= H) | (lane <= row), top, 0.0)
    low = jnp.where(lane < H, 0.0, D[H:, :]) - mm(top[:, H:], top, 0, 0)
    low = reduce_half([low[8 * i:8 * i + 8, :] for i in range(H // 8)], H)
    return jnp.concatenate(
        [jnp.where(lane < H, top, 0.0), jnp.where(lane <= row + H, low, 0.0)], axis=0)


def add_diag(square, row):
    r = lax.broadcasted_iota(jnp.int32, square.shape, 0)
    c = lax.broadcasted_iota(jnp.int32, square.shape, 1)
    return square + jnp.where(r == c, row, 0.0)


def tree_kernel(
    sizes, blocks_ref, block_res_ref, owner_ref, leaf_prior_ref, node_rows_ref, node_res_ref, node_prior_ref,
    interior_ref, own_ref,
    t_ref, inv_ref, base_ref, g2_ref, s_ref, c_ref, in_s, in_c, step_ref, u_ref, f_ref,
    shift_ref, gain_ref, land_ref, j1_ref, leaf_send, leaf_recv, up_send, up_recv, down_send, down_recv,
    early_send, early_recv, rows_ref, res_ref, land_res_ref, res_send, res_recv, z_ref,
):
    grp_count, sub_count = sizes
    count = grp_count * sub_count
    depth = count.bit_length() - 1
    pos = lax.axis_index("grp") * sub_count + lax.axis_index("sub")
    odd = pos % 2 == 1
    even = pos % 2 == 0
    middle = count // 2 - 1
    top = pos == count - 1
    root = pos == middle
    below_root = pos != middle
    odd_node = odd & (pos != count - 1)
    below_top = pos != count - 1
    stride = jnp.int32(0)
    left = jnp.int32(0)
    for level in range(1, depth + 2):
        here = jnp.where((pos + 1) % 2**level == 2 ** (level - 1), 1, 0)
        stride = stride + here * 2 ** (level - 1)
        left = left + here * (1 - (pos + 1) // 2**level % 2)
    parent = jnp.where(top, middle, pos + (2 * left - 1) * stride)
    parent = jnp.where(root, count - 1, parent)
    to_slot = jnp.where(top, 2, 1 - left)
    half = stride // 2

    def device(target):
        return (target // sub_count, target % sub_count)

    def up_copy(phase, n, target, slot):
        if n == NB:
            src, dst = c_ref.at[phase], in_c.at[slot]
        else:
            at = (pl.ds(B * n, B), pl.ds(B * n, W - B * n))
            if n == 0:
                at = (pl.ds(0, B), pl.ds(0, B))
            if n == NB + 1:
                at = (pl.ds(0, B), pl.ds(B, W - B))
            src, dst = s_ref.at[phase, at[0], at[1]], in_s.at[slot, at[0], at[1]]
        return pltpu.make_async_remote_copy(
            src_ref=src, dst_ref=dst, send_sem=up_send.at[phase, n],
            recv_sem=up_recv.at[slot, n], device_id=device(target), device_id_type=MESH)

    def down_copy(dst, n, r, target):
        return pltpu.make_async_remote_copy(
            src_ref=step_ref, dst_ref=dst, send_sem=down_send.at[n], recv_sem=down_recv.at[r],
            device_id=device(target), device_id_type=MESH)

    def early_copy(n):
        src = (base_ref.at[1], t_ref.at[1, :, pl.ds(W, W)], g2_ref.at[1])[n]
        dst = (in_s.at[0], in_s.at[2], in_c.at[0])[n]
        return pltpu.make_async_remote_copy(
            src_ref=src, dst_ref=dst, send_sem=early_send.at[n], recv_sem=early_recv.at[n],
            device_id=device(jnp.where(root, count - 1, middle)), device_id_type=MESH)

    some_other = jnp.where(odd, pos - 1, pos + 1)

    def rows_of(k):
        return slice(B * k, B * k + B)

    group = lax.axis_index("grp")
    place = lax.axis_index("sub")
    slot_rows = 2 * blocks_ref.shape[0] // sub_count * blocks_ref.shape[1]
    per_block = B // slot_rows

    def peer_of(j):
        peer = place
        for bit in range(sub_count.bit_length() - 1):
            if j >> bit & 1:
                peer = peer + 2**bit * (1 - 2 * (place // 2**bit % 2))
        return peer

    def leaf_copy(j):
        peer = peer_of(j)
        return pltpu.make_async_remote_copy(
            src_ref=rows_ref.at[peer], dst_ref=land_ref.at[j], send_sem=leaf_send.at[j],
            recv_sem=leaf_recv.at[j], device_id=(group, peer), device_id_type=MESH)

    def res_copy(j):
        return pltpu.make_async_remote_copy(
            src_ref=res_ref.at[j], dst_ref=land_res_ref.at[j], send_sem=res_send.at[j],
            recv_sem=res_recv.at[j], device_id=(group, peer_of(j)), device_id_type=MESH)

    block_list, per, columns = blocks_ref.shape
    held = block_list * per
    f32, bf16 = jnp.float32, jnp.bfloat16

    def grid(shape, dim):
        return lax.broadcasted_iota(jnp.int32, shape, dim)

    def many(row):
        return jnp.broadcast_to(row, (16, row.shape[1])).astype(bf16)

    repeat = jnp.where(
        grid((block_list, held), 1) // per == grid((block_list, held), 0), 1.0, 0.0
    ).astype(bf16)
    earlier = jnp.where(
        grid((block_list, block_list), 0) < grid((block_list, block_list), 1), 1.0, 0.0
    ).astype(bf16)
    kinds = max(sub_count, 16)
    names = jnp.where(grid((kinds, block_list), 0) == owner_ref[0:1, :], 1.0, 0.0)
    ahead_of = jnp.sum(mm16(names.astype(bf16), earlier, 1, 0) * names, axis=0, keepdims=True)
    rank = mm16(many(ahead_of), repeat, 1, 0)[0:1, :]
    named = mm16(many(owner_ref[0:1, :].astype(f32)), repeat, 1, 0)[0:1, :]
    at_row = (rank * per).astype(jnp.int32) + grid((1, held), 1) % per
    named = named.astype(jnp.int32)
    spread = mm16(
        jnp.concatenate([block_res_ref[...].astype(f32), jnp.zeros((16 - per, block_list), f32)], axis=0).astype(bf16),
        repeat, 1, 0,
    )
    spread = jnp.where(grid((16, held), 0) == grid((16, held), 1) % per, spread, 0.0)
    line_res = many(jnp.sum(spread, axis=0, keepdims=True))
    for j in range(sub_count):
        hit = grid((B, held), 0) == at_row + (j % per_block) * slot_rows
        hit = jnp.where(hit & (named == peer_of(j)), 1.0, 0.0).astype(bf16)
        res_ref[j] = mm16(line_res, hit, 1, 1).astype(bf16)
        if j > 0:
            res_copy(j).start()

    table = jnp.where(
        grid((sub_count * slot_rows, held), 0) == named * slot_rows + at_row, 1.0, 0.0
    ).astype(bf16)
    placed = mm16(table, blocks_ref[...].reshape(held, columns), 1, 0)
    for n in range(sub_count):
        rows_ref[n] = placed[slot_rows * n:slot_rows * (n + 1), :].astype(bf16)
    for j in range(1, sub_count):
        leaf_copy(j).start()

    def arrive(k):
        rows = rows_of(k)
        parts = []
        values = jnp.zeros((16, B), f32)
        for j in range(per_block * k, per_block * k + per_block):
            if j == 0:
                parts.append(rows_ref[place].astype(f32))
                values = values + res_ref[0].astype(f32)
            else:
                leaf_copy(j).wait_recv()
                res_copy(j).wait_recv()
                parts.append(land_ref[j].astype(f32))
                values = values + land_res_ref[j].astype(f32)
        block = jnp.concatenate(parts, axis=0)
        t_ref[0, rows, W:2 * W] = block[:, NI:]
        z_ref[0, :, rows] = values[0:8, :]
        line = block[:, :NI]
        j1_ref[rows, :] = line.astype(jnp.bfloat16)
        above = j1_ref[:B * k + B, :]
        scaled = thirds(line * (1.0 / leaf_prior_ref[0:1, :NI]))
        square = mm16(above, scaled[2], 1, 1) + mm16(above, scaled[1], 1, 1)
        square = square + mm16(above, scaled[0], 1, 1)
        for i in range(k):
            part = square[rows_of(i), :]
            if i > 0:
                part = part - mm(t_ref[0, :B * i, rows_of(i)], t_ref[0, :B * i, rows], 0, 0)
            if i < k - 1:
                part = mm(inv_ref[0, rows_of(i), :], part, 1, 0)
            t_ref[0, rows_of(i), rows] = part
        corner = add_diag(square[rows, :], jnp.float32(1.0))
        if k > 1:
            corner = corner - mm(t_ref[0, :B * k - B, rows], t_ref[0, :B * k - B, rows], 0, 0)
        t_ref[0, rows, rows] = corner

    r1 = node_rows_ref[:, :W]
    r2 = node_rows_ref[:, W:]
    res = jnp.broadcast_to(node_res_ref[0:1, :], (16, node_res_ref.shape[1]))
    t_ref[1, :, :W] = add_diag(mm16(r1, r1, 0, 0), node_prior_ref[0:1, :W])

    @pl.when(root)
    def _():
        t_ref[1, :, W:2 * W] = mm16(r2, r1, 0, 0)

    @pl.when(below_root)
    def _():
        t_ref[1, :, W:2 * W] = mm16(r1, r2, 0, 0)

    base_ref[1] = jnp.where(top, 0.0, add_diag(mm16(r2, r2, 0, 0), node_prior_ref[0:1, W:]))
    step_ref[...] = mm16(res, r1, 1, 0)[0:8, :]
    g2_ref[1] = jnp.where(top, 0.0, mm16(res, r2, 1, 0)[0:8, :])

    @pl.when(root)
    def _():
        for n in range(3):
            early_copy(n).start()

    t_ref[0, :, :W] = jnp.zeros((W, W), jnp.float32)
    base_ref[0] = add_diag(jnp.zeros((W, W), jnp.float32), leaf_prior_ref[0:1, NI:])
    g2_ref[0] = jnp.zeros((8, W), jnp.float32)

    def back(phase, first):
        for k in range(NB - 1, -1, -1):
            line = z_ref[phase, :, rows_of(k)]
            rest = slice(B * k + B, W)
            if k < NB - 1:
                line = line - mm(shift_ref[phase, :, rest], t_ref[phase, rows_of(k), rest], 1, 1)
            shift_ref[phase, :, rows_of(k)] = mm(line, inv_ref[phase, rows_of(k), :], 1, 0)
            if first < 2 * W:
                right = t_ref[phase, rows_of(k), first:]
                if k < NB - 1:
                    right = right - mm(
                        t_ref[phase, rows_of(k), rest], t_ref[phase, rest, first:], 1, 0
                    )
                t_ref[phase, rows_of(k), first:] = mm(inv_ref[phase, rows_of(k), :], right, 0, 0)
        if first < 2 * W:
            for n, part in enumerate(thirds(t_ref[phase, :, W:2 * W])):
                gain_ref[phase, n] = part

    def stacked(row):
        return jnp.concatenate([x for x in thirds(jnp.concatenate([row, row], axis=0))], axis=0)

    def unstacked(total):
        return total[32:40] + total[16:24] + total[0:8]

    def less_gain(phase, row):
        stack = stacked(row)
        total = mm16(stack, gain_ref[phase, 2], 1, 1) + mm16(stack, gain_ref[phase, 1], 1, 1)
        total = total + mm16(stack, gain_ref[phase, 0], 1, 1)
        return shift_ref[phase] - unstacked(total)

    def receive(k):
        if k == 0:

            @pl.when(odd)
            def _():
                back(0, W)

            @pl.when(root)
            def _():
                for n in range(3):
                    early_copy(n).wait_send()

            @pl.when(top)
            def _():
                for n in range(3):
                    early_copy(n).wait_recv()
                step_ref[...] += in_c[0]
                t_ref[1, :, :W] += in_s[0]
                t_ref[1, :, W:2 * W] = in_s[2]

        if k == 1:

            @pl.when(odd_node)
            def _():
                up_copy(0, NB, some_other, 0).wait_recv()
                step_ref[...] += in_c[0]

            @pl.when(even)
            def _():
                step_ref[...] += c_ref[0]

            @pl.when(below_top)
            def _():
                up_copy(0, NB, some_other, 1).wait_recv()
                step_ref[...] += in_c[1]

            @pl.when(root)
            def _():
                up_copy(0, NB, some_other, 2).wait_recv()
                step_ref[...] += in_c[2]

            z_ref[1] = step_ref[...]

        pieces = [(k, rows_of(k), slice(B * k, B if k == 0 else W))]
        if k == 1:
            pieces = [(NB + 1, rows_of(0), slice(B, W))] + pieces

        for n, rows, cols in pieces:

            @pl.when(odd_node)
            def _():
                up_copy(0, n, some_other, 0).wait_recv()
                t_ref[1, rows, cols] += in_s[0, rows, cols]

            @pl.when(even)
            def _():
                t_ref[1, rows, cols] += s_ref[0, rows, cols]

            @pl.when(below_top)
            def _():
                up_copy(0, n, some_other, 1).wait_recv()
                t_ref[1, rows, cols] += in_s[1, rows, cols]

            @pl.when(root)
            def _():
                up_copy(0, n, some_other, 2).wait_recv()
                t_ref[1, rows, cols] += in_s[2, rows, cols]

    def eliminate(phase, _):
        sign = jnp.where(phase == 0, 1.0, -1.0).astype(jnp.float32)
        for k in range(NB):
            rows = rows_of(k)
            pl.when(phase == 0)(lambda: arrive(k))
            pl.when(phase == 1)(lambda: receive(k))
            block = t_ref[phase, rows, rows]
            if k > 0:
                before = rows_of(k - 1)
                inv = inv_ref[phase, before, :]
                near = mm(inv, t_ref[phase, before, rows], 1, 0)
                t_ref[phase, before, rows] = near
                block = block - mm(near, near, 0, 0)
                col = t_ref[phase, :B * k, rows]
                far = slice(B * k + B, 2 * W)
                t_ref[phase, before, far] = mm(inv, t_ref[phase, before, far], 1, 0)
                t_ref[phase, rows, far] -= mm(col, t_ref[phase, :B * k, far], 0, 0)
                z_ref[phase, :, before] = mm(z_ref[phase, :, before], inv, 1, 1)
                z_ref[phase, :, rows] -= mm(z_ref[phase, :, :B * k], col, 1, 0)
                if k < NB - 1:
                    after = rows_of(k + 1)
                    ahead = t_ref[phase, :B * k, after]
                    t_ref[phase, after, after] -= mm(ahead, ahead, 0, 0)
            if k >= 2:
                for n in range(NB):
                    y = t_ref[phase, (0 if k == 2 else 2 * B):B * k, W:2 * W]
                    base_ref[phase, rows_of(n), B * n:] += sign * mm(
                        y[:, rows_of(n)], y[:, B * n:], 0, 0
                    )
            inv_ref[phase, rows, :] = inverse_factor(block)
        rows = rows_of(NB - 1)

        target = jnp.where(phase == 0, some_other, parent)
        slot = jnp.where(phase == 0, 1, to_slot)
        sends = jnp.where(phase == 0, odd, below_root)

        def finish(n, cols):
            y = t_ref[phase, rows, W:2 * W]
            r = rows_of(n % (NB + 1))
            s_ref[phase, r, cols] = base_ref[phase, r, cols] + sign * mm(y[:, r], y[:, cols], 0, 0)

        def push(n):
            @pl.when(sends)
            def _():
                up_copy(phase, n, target, slot).start()

        inv = inv_ref[phase, rows, :]
        first = mm(inv, t_ref[phase, rows, W:W + B], 1, 0)
        t_ref[phase, rows, W:W + B] = first
        s_ref[phase, :B, :B] = base_ref[phase, :B, :B] + sign * mm(first, first, 0, 0)
        push(0)
        t_ref[phase, rows, W + B:2 * W] = mm(inv, t_ref[phase, rows, W + B:2 * W], 1, 0)
        finish(NB + 1, slice(B, W))
        push(NB + 1)
        z_ref[phase, :, rows] = mm(z_ref[phase, :, rows], inv, 1, 1)
        c_ref[phase] = g2_ref[phase] + sign * mm(z_ref[phase], t_ref[phase, :, W:2 * W], 1, 0)
        push(NB)
        for n in range(1, NB):
            finish(n, slice(B * n, W))
            push(n)

        return 0

    lax.fori_loop(0, 2, eliminate, 0)

    @pl.when(below_root)
    def _():
        back(1, W)

        @pl.when(even)
        def _():
            back(0, W)

        down_copy(u_ref, 0, 0, parent).wait_recv()
        step_ref[...] = less_gain(1, u_ref[...])

    @pl.when(root)
    def _():
        back(1, 2 * W)
        step_ref[...] = shift_ref[1]
        down_copy(u_ref, 3, 0, count - 1).start()

    @pl.when(odd_node)
    def _():
        down_copy(u_ref, 0, 0, pos - half).start()
        down_copy(u_ref, 1, 0, pos + half).start()

    @pl.when(odd)
    def _():
        down_copy(f_ref, 2, 1, some_other).wait_recv()

    @pl.when(even)
    def _():
        down_copy(f_ref, 2, 1, some_other).start()
        f_ref[...] = step_ref[...]

    own_ref[...] = step_ref[0:1, :]
    line = unstacked(mm16(stacked(less_gain(0, f_ref[...])), j1_ref[...], 1, 0))
    interior_ref[...] = line[0:1, :] / leaf_prior_ref[0:1, :NI]

    for j in range(1, sub_count):
        leaf_copy(j).wait_send()
        res_copy(j).wait_send()

    @pl.when(odd)
    def _():
        for n in range(NB + 2):
            up_copy(0, n, some_other, 1).wait_send()

    @pl.when(odd_node)
    def _():
        down_copy(u_ref, 0, 0, pos - half).wait_send()
        down_copy(u_ref, 1, 0, pos + half).wait_send()

    @pl.when(root)
    def _():
        down_copy(u_ref, 3, 0, count - 1).wait_send()

    @pl.when(even)
    def _():
        down_copy(f_ref, 2, 1, some_other).wait_send()

    @pl.when(below_root)
    def _():
        for n in range(NB + 2):
            up_copy(1, n, parent, to_slot).wait_send()


def shards(
    sizes,
    measurement_block_rows,
    measurement_residual,
    owner,
    submap_prior_weight,
    separator_measure_rows,
    separator_residual,
    separator_prior_weight,
):
    sub_count = sizes[1]
    block_list, rows_per_block, column_count = measurement_block_rows.shape
    slot_rows = 2 * block_list // sub_count * rows_per_block
    vmem = pl.BlockSpec(memory_space=pltpu.VMEM)
    f32 = jnp.float32
    interior, own = pl.pallas_call(
        lambda *refs: tree_kernel(sizes, *refs),
        out_shape=(
            jax.ShapeDtypeStruct((1, NI), f32),
            jax.ShapeDtypeStruct((1, W), f32),
        ),
        in_specs=[vmem] * 7,
        out_specs=(vmem, vmem),
        scratch_shapes=[
            pltpu.VMEM((2, W, 2 * W), f32),
            pltpu.VMEM((2, W, B), f32),
            pltpu.VMEM((2, W, W), f32),
            pltpu.VMEM((2, 8, W), f32),
            pltpu.VMEM((2, W, W), f32),
            pltpu.VMEM((2, 8, W), f32),
            pltpu.VMEM((3, W, W), f32),
            pltpu.VMEM((3, 8, W), f32),
            pltpu.VMEM((8, W), f32),
            pltpu.VMEM((8, W), f32),
            pltpu.VMEM((8, W), f32),
            pltpu.VMEM((2, 8, W), f32),
            pltpu.VMEM((2, 3, W, W), jnp.bfloat16),
            pltpu.VMEM((sub_count, slot_rows, column_count), jnp.bfloat16),
            pltpu.VMEM((W, NI), jnp.bfloat16),
            pltpu.SemaphoreType.DMA((sub_count,)),
            pltpu.SemaphoreType.DMA((sub_count,)),
            pltpu.SemaphoreType.DMA((2, NB + 2)),
            pltpu.SemaphoreType.DMA((3, NB + 2)),
            pltpu.SemaphoreType.DMA((4,)),
            pltpu.SemaphoreType.DMA((2,)),
            pltpu.SemaphoreType.DMA((3,)),
            pltpu.SemaphoreType.DMA((3,)),
            pltpu.VMEM((sub_count, slot_rows, column_count), jnp.bfloat16),
            pltpu.VMEM((sub_count, 16, B), jnp.bfloat16),
            pltpu.VMEM((sub_count, 16, B), jnp.bfloat16),
            pltpu.SemaphoreType.DMA((sub_count,)),
            pltpu.SemaphoreType.DMA((sub_count,)),
            pltpu.VMEM((2, 8, W), f32),
        ],
        compiler_params=pltpu.CompilerParams(
            has_side_effects=True, vmem_limit_bytes=56 * 2**20
        ),
    )(
        measurement_block_rows,
        measurement_residual.T,
        owner.T,
        submap_prior_weight,
        separator_measure_rows,
        separator_residual,
        separator_prior_weight,
    )

    def pass_on(a_ref, b_ref, a_out, b_out):
        a_out[...] = a_ref[...]
        b_out[...] = b_ref[...]

    return tuple(pl.pallas_call(
        pass_on,
        out_shape=(jax.ShapeDtypeStruct((1, NI), f32), jax.ShapeDtypeStruct((1, W), f32)),
        in_specs=[vmem] * 2,
        out_specs=(vmem, vmem),
    )(interior, own))


def solution(mesh):
    sizes = (mesh.shape["grp"], mesh.shape["sub"])
    return jax.shard_map(
        lambda *args: shards(sizes, *args),
        mesh=mesh,
        in_specs=(
            P(("grp", "sub"), None, None),
            P(("grp", "sub"), None),
            P(("grp", "sub"), None),
            P(("grp", "sub"), None),
            P(("grp", "sub"), None),
            P(("grp", "sub"), None),
            P(("grp", "sub"), None),
        ),
        out_specs=(P(("grp", "sub"), None), P(("grp", "sub"), None)),
        check_vma=False,
    )
```

```python
import jax
import jax.numpy as jnp
from jax import lax
from jax.experimental import pallas as pl
from jax.experimental.pallas import tpu as pltpu
from jax.sharding import PartitionSpec as P

NI = 1024
W = 512
B = 128
NB = W // B
MESH = pl.DeviceIdType.MESH
highest = lax.Precision.HIGHEST


def mm(a, b, ca, cb):
    return lax.dot_general(
        a, b, (((ca,), (cb,)), ((), ())), precision=highest, preferred_element_type=jnp.float32
    )


def mm16(a, b, ca, cb):
    return lax.dot_general(a, b, (((ca,), (cb,)), ((), ())), preferred_element_type=jnp.float32)


def thirds(x):
    hi = x.astype(jnp.bfloat16)
    rest = x - hi.astype(jnp.float32)
    mid = rest.astype(jnp.bfloat16)
    low = (rest - mid.astype(jnp.float32)).astype(jnp.bfloat16)
    return hi, mid, low


def lane_spread(v, j):
    return jnp.broadcast_to(v[:, j:j + 1], (8, B))


def row_spread(v, i):
    return jnp.broadcast_to(v[i:i + 1, :], (8, B))


def pivot_pair(C, k):
    h, i = k // 8, k % 8
    X, Y = C[h][k], C[h][k + 1]
    a, b, c = row_spread(X, i), row_spread(X, i + 1), row_spread(Y, i + 1)
    r = 1.0 / (a * c - b * b)
    N, M = {}, {}
    for g in range(h, 2):
        Xg, Yg = C[g][k], C[g][k + 1]
        N[g] = (Xg * c - Yg * b, Yg * a - Xg * b)
        M[g] = (N[g][0] * r, N[g][1] * r)
    m = {}
    for j in range(k + 2, 16):
        hj = j // 8
        m[j] = (row_spread(M[hj][0], j % 8), row_spread(M[hj][1], j % 8))
        if j < k + 4:
            x, y = row_spread(C[hj][k], j % 8), row_spread(C[hj][k + 1], j % 8)
            for g in range(hj, 2):
                C[g][j] = C[g][j] - r * (N[g][0] * x + N[g][1] * y)
        else:
            for g in range(hj, 2):
                C[g][j] = C[g][j] - (C[g][k] * m[j][0] + C[g][k + 1] * m[j][1])
    return (a, b, c, r), m


def scaled_rows(u, pairs, sub):
    def join(parts, step):
        total = parts[0]
        for n in range(1, len(parts)):
            total = jnp.where(sub >= n * step, parts[n], total)
        return total

    a, b, r = (join([p[0][n] for p in pairs], 2) for n in (0, 1, 3))
    U, V = join(u, 1), join(u[0::2], 2)
    ra = lax.rsqrt(a)
    d = a * r
    return jnp.where(sub % 2 == 1, (U - (b * (ra * ra)) * V) * (d * lax.rsqrt(d)), U * ra)


def reduce_half(T, off):
    lane = lax.broadcasted_iota(jnp.int32, (8, B), 1)
    sub = lax.broadcasted_iota(jnp.int32, (8, B), 0)
    T = list(T)
    out = []
    n = len(T)
    for t in range(0, n, 2):
        la = off + 8 * t
        C = [[lane_spread(T[t], la + k) for k in range(8)],
             [lane_spread(T[t + 1], la + k) for k in range(16)]]
        cs = {i: [lane_spread(T[i], la + k) for k in range(8)] for i in range(t + 2, n)}
        cs[t + 1] = C[1][:8]
        pairs = [pivot_pair(C, k) for k in range(0, 16, 2)]
        for h in range(2):
            l = la + 8 * h
            inside = (lane >= l) & (lane < l + 8)
            base = jnp.where(inside, jnp.where(lane == sub + l, 1.0, 0.0), T[t + h])
            u = [row_spread(base, k) for k in range(8)]
            four = pairs[4 * h:4 * h + 4]
            for k in range(0, 6, 2):
                for i in range(k + 2, 8):
                    m = four[k // 2][1][i + 8 * h]
                    u[i] = u[i] - (m[0] * u[k] + m[1] * u[k + 1])
            out.append(scaled_rows(u, four, sub))
            if t + h + 1 == n:
                break
            q = [None] * 8
            for k in range(6, -1, -2):
                a, b, c, r = four[k // 2][0]
                q[k] = (c * u[k] - b * u[k + 1]) * r
                q[k + 1] = (a * u[k + 1] - b * u[k]) * r
            for k in range(6, 0, -2):
                for i in range(k):
                    m, m1 = four[i // 2][1][k + 8 * h][i % 2], four[i // 2][1][k + 1 + 8 * h][i % 2]
                    q[i] = q[i] - (m * q[k] + m1 * q[k + 1])
            for i in range(t + h + 1, n):
                if h == 1:
                    cs[i] = [lane_spread(T[i], l + k) for k in range(8)]
                p = [cs[i][k] * q[k] for k in range(8)]
                T[i] = jnp.where(inside, 0.0, T[i]) - (
                    ((p[0] + p[1]) + (p[2] + p[3])) + ((p[4] + p[5]) + (p[6] + p[7])))
    return jnp.concatenate(out, axis=0)


def inverse_factor(D):
    H = B // 2
    lane = lax.broadcasted_iota(jnp.int32, (H, B), 1)
    row = lax.broadcasted_iota(jnp.int32, (H, B), 0)
    top = reduce_half([D[8 * i:8 * i + 8, :] for i in range(H // 8)], 0)
    top = jnp.where((lane >= H) | (lane <= row), top, 0.0)
    low = jnp.where(lane < H, 0.0, D[H:, :]) - mm(top[:, H:], top, 0, 0)
    low = reduce_half([low[8 * i:8 * i + 8, :] for i in range(H // 8)], H)
    return jnp.concatenate(
        [jnp.where(lane < H, top, 0.0), jnp.where(lane <= row + H, low, 0.0)], axis=0)


def add_diag(square, row):
    r = lax.broadcasted_iota(jnp.int32, square.shape, 0)
    c = lax.broadcasted_iota(jnp.int32, square.shape, 1)
    return square + jnp.where(r == c, row, 0.0)


def tree_kernel(
    sizes, blocks_ref, block_res_ref, owner_ref, leaf_prior_ref, node_rows_ref, node_res_ref, node_prior_ref,
    interior_ref, own_ref,
    t_ref, inv_ref, base_ref, g2_ref, s_ref, c_ref, in_s, in_c, step_ref, u_ref, f_ref,
    shift_ref, gain_ref, land_ref, j1_ref, leaf_send, leaf_recv, up_send, up_recv, down_send, down_recv,
    early_send, early_recv, rows_ref, res_ref, land_res_ref, res_send, res_recv, z_ref, side_ref,
):
    grp_count, sub_count = sizes
    count = grp_count * sub_count
    depth = count.bit_length() - 1
    pos = lax.axis_index("grp") * sub_count + lax.axis_index("sub")
    odd = pos % 2 == 1
    even = pos % 2 == 0
    middle = count // 2 - 1
    top = pos == count - 1
    root = pos == middle
    below_root = pos != middle
    odd_node = odd & (pos != count - 1)
    below_top = pos != count - 1
    stride = jnp.int32(0)
    left = jnp.int32(0)
    for level in range(1, depth + 2):
        here = jnp.where((pos + 1) % 2**level == 2 ** (level - 1), 1, 0)
        stride = stride + here * 2 ** (level - 1)
        left = left + here * (1 - (pos + 1) // 2**level % 2)
    parent = jnp.where(top, middle, pos + (2 * left - 1) * stride)
    parent = jnp.where(root, count - 1, parent)
    to_slot = jnp.where(top, 2, 1 - left)
    half = stride // 2

    def device(target):
        return (target // sub_count, target % sub_count)

    def up_copy(phase, n, target, slot):
        if n == NB:
            src, dst = c_ref.at[phase], in_c.at[slot]
        else:
            at = (pl.ds(B * n, B), pl.ds(B * n, W - B * n))
            if n == 0:
                at = (pl.ds(0, B), pl.ds(0, B))
            if n == NB + 1:
                at = (pl.ds(0, B), pl.ds(B, W - B))
            src, dst = s_ref.at[phase, at[0], at[1]], in_s.at[slot, at[0], at[1]]
        return pltpu.make_async_remote_copy(
            src_ref=src, dst_ref=dst, send_sem=up_send.at[phase, n],
            recv_sem=up_recv.at[slot, n], device_id=device(target), device_id_type=MESH)

    def down_copy(dst, n, r, target):
        return pltpu.make_async_remote_copy(
            src_ref=step_ref, dst_ref=dst, send_sem=down_send.at[n], recv_sem=down_recv.at[r],
            device_id=device(target), device_id_type=MESH)

    def early_copy(n):
        src = (base_ref.at[1], t_ref.at[1, :, pl.ds(W, W)], g2_ref.at[1])[n]
        dst = (in_s.at[0], in_s.at[2], in_c.at[0])[n]
        return pltpu.make_async_remote_copy(
            src_ref=src, dst_ref=dst, send_sem=early_send.at[n], recv_sem=early_recv.at[n],
            device_id=device(jnp.where(root, count - 1, middle)), device_id_type=MESH)

    some_other = jnp.where(odd, pos - 1, pos + 1)

    def rows_of(k):
        return slice(B * k, B * k + B)

    group = lax.axis_index("grp")
    place = lax.axis_index("sub")
    slot_rows = 2 * blocks_ref.shape[0] // sub_count * blocks_ref.shape[1]
    per_block = B // slot_rows

    def peer_of(j):
        peer = place
        for bit in range(sub_count.bit_length() - 1):
            if j >> bit & 1:
                peer = peer + 2**bit * (1 - 2 * (place // 2**bit % 2))
        return peer

    def leaf_copy(j):
        peer = peer_of(j)
        return pltpu.make_async_remote_copy(
            src_ref=rows_ref.at[peer], dst_ref=land_ref.at[j], send_sem=leaf_send.at[j],
            recv_sem=leaf_recv.at[j], device_id=(group, peer), device_id_type=MESH)

    def res_copy(j):
        return pltpu.make_async_remote_copy(
            src_ref=res_ref.at[j], dst_ref=land_res_ref.at[j], send_sem=res_send.at[j],
            recv_sem=res_recv.at[j], device_id=(group, peer_of(j)), device_id_type=MESH)

    block_list, per, columns = blocks_ref.shape
    held = block_list * per
    f32, bf16 = jnp.float32, jnp.bfloat16

    def grid(shape, dim):
        return lax.broadcasted_iota(jnp.int32, shape, dim)

    def many(row):
        return jnp.broadcast_to(row, (16, row.shape[1])).astype(bf16)

    repeat = jnp.where(
        grid((block_list, held), 1) // per == grid((block_list, held), 0), 1.0, 0.0
    ).astype(bf16)
    earlier = jnp.where(
        grid((block_list, block_list), 0) < grid((block_list, block_list), 1), 1.0, 0.0
    ).astype(bf16)
    kinds = max(sub_count, 16)
    names = jnp.where(grid((kinds, block_list), 0) == owner_ref[0:1, :], 1.0, 0.0)
    ahead_of = jnp.sum(mm16(names.astype(bf16), earlier, 1, 0) * names, axis=0, keepdims=True)
    rank = mm16(many(ahead_of), repeat, 1, 0)[0:1, :]
    named = mm16(many(owner_ref[0:1, :].astype(f32)), repeat, 1, 0)[0:1, :]
    at_row = (rank * per).astype(jnp.int32) + grid((1, held), 1) % per
    named = named.astype(jnp.int32)
    spread = mm16(
        jnp.concatenate([block_res_ref[...].astype(f32), jnp.zeros((16 - per, block_list), f32)], axis=0).astype(bf16),
        repeat, 1, 0,
    )
    spread = jnp.where(grid((16, held), 0) == grid((16, held), 1) % per, spread, 0.0)
    line_res = many(jnp.sum(spread, axis=0, keepdims=True))
    for j in range(sub_count):
        hit = grid((B, held), 0) == at_row + (j % per_block) * slot_rows
        hit = jnp.where(hit & (named == peer_of(j)), 1.0, 0.0).astype(bf16)
        res_ref[j] = mm16(line_res, hit, 1, 1).astype(bf16)
        if j > 0:
            res_copy(j).start()

    table = jnp.where(
        grid((sub_count * slot_rows, held), 0) == named * slot_rows + at_row, 1.0, 0.0
    ).astype(bf16)
    placed = mm16(table, blocks_ref[...].reshape(held, columns), 1, 0)
    for n in range(sub_count):
        rows_ref[n] = placed[slot_rows * n:slot_rows * (n + 1), :].astype(bf16)
    for j in range(1, sub_count):
        leaf_copy(j).start()

    def arrive(k):
        rows = rows_of(k)
        parts = []
        values = jnp.zeros((16, B), f32)
        for j in range(per_block * k, per_block * k + per_block):
            if j == 0:
                parts.append(rows_ref[place].astype(f32))
                values = values + res_ref[0].astype(f32)
            else:
                leaf_copy(j).wait_recv()
                res_copy(j).wait_recv()
                parts.append(land_ref[j].astype(f32))
                values = values + land_res_ref[j].astype(f32)
        block = jnp.concatenate(parts, axis=0)
        t_ref[0, rows, W:2 * W] = block[:, NI:]
        z_ref[0, :, rows] = values[0:8, :]
        line = block[:, :NI]
        j1_ref[rows, :] = line.astype(jnp.bfloat16)
        above = j1_ref[:B * k + B, :]
        scaled = thirds(line * (1.0 / leaf_prior_ref[0:1, :NI]))
        square = mm16(above, scaled[2], 1, 1) + mm16(above, scaled[1], 1, 1)
        square = square + mm16(above, scaled[0], 1, 1)
        for i in range(k):
            part = square[rows_of(i), :]
            if i > 0:
                part = part - mm(t_ref[0, :B * i, rows_of(i)], t_ref[0, :B * i, rows], 0, 0)
            if i < k - 1:
                part = mm(inv_ref[0, rows_of(i), :], part, 1, 0)
            t_ref[0, rows_of(i), rows] = part
            if i == k - 1:
                side_ref[...] = part.T
        corner = add_diag(square[rows, :], jnp.float32(1.0))
        if k > 1:
            corner = corner - mm(t_ref[0, :B * k - B, rows], t_ref[0, :B * k - B, rows], 0, 0)
        t_ref[0, rows, rows] = corner

    r1 = node_rows_ref[:, :W]
    r2 = node_rows_ref[:, W:]
    res = jnp.broadcast_to(node_res_ref[0:1, :], (16, node_res_ref.shape[1]))
    t_ref[1, :, :W] = add_diag(mm16(r1, r1, 0, 0), node_prior_ref[0:1, :W])

    @pl.when(root)
    def _():
        t_ref[1, :, W:2 * W] = mm16(r2, r1, 0, 0)

    @pl.when(below_root)
    def _():
        t_ref[1, :, W:2 * W] = mm16(r1, r2, 0, 0)

    base_ref[1] = jnp.where(top, 0.0, add_diag(mm16(r2, r2, 0, 0), node_prior_ref[0:1, W:]))
    step_ref[...] = mm16(res, r1, 1, 0)[0:8, :]
    g2_ref[1] = jnp.where(top, 0.0, mm16(res, r2, 1, 0)[0:8, :])

    @pl.when(root)
    def _():
        for n in range(3):
            early_copy(n).start()

    t_ref[0, :, :W] = jnp.zeros((W, W), jnp.float32)
    base_ref[0] = add_diag(jnp.zeros((W, W), jnp.float32), leaf_prior_ref[0:1, NI:])
    g2_ref[0] = jnp.zeros((8, W), jnp.float32)

    def back(phase, first):
        for k in range(NB - 1, -1, -1):
            line = z_ref[phase, :, rows_of(k)]
            rest = slice(B * k + B, W)
            if k < NB - 1:
                line = line - mm(shift_ref[phase, :, rest], t_ref[phase, rows_of(k), rest], 1, 1)
            shift_ref[phase, :, rows_of(k)] = mm(line, inv_ref[phase, rows_of(k), :], 1, 0)
            if first < 2 * W:
                right = t_ref[phase, rows_of(k), first:]
                if k < NB - 1:
                    right = right - mm(
                        t_ref[phase, rows_of(k), rest], t_ref[phase, rest, first:], 1, 0
                    )
                t_ref[phase, rows_of(k), first:] = mm(inv_ref[phase, rows_of(k), :], right, 0, 0)
        if first < 2 * W:
            for n, part in enumerate(thirds(t_ref[phase, :, W:2 * W].T)):
                gain_ref[phase, n] = part

    def stacked(row):
        return jnp.concatenate([x for x in thirds(jnp.concatenate([row, row], axis=0))], axis=0)

    def unstacked(total):
        return total[32:40] + total[16:24] + total[0:8]

    def less_gain(phase, row):
        stack = stacked(row)
        total = mm16(stack, gain_ref[phase, 2], 1, 0) + mm16(stack, gain_ref[phase, 1], 1, 0)
        total = total + mm16(stack, gain_ref[phase, 0], 1, 0)
        return shift_ref[phase] - unstacked(total)

    def receive(k):
        if k == 0:

            @pl.when(odd)
            def _():
                back(0, W)

            @pl.when(root)
            def _():
                for n in range(3):
                    early_copy(n).wait_send()

            @pl.when(top)
            def _():
                for n in range(3):
                    early_copy(n).wait_recv()
                step_ref[...] += in_c[0]
                t_ref[1, :, :W] += in_s[0]
                t_ref[1, :, W:2 * W] = in_s[2]

        if k == 1:

            @pl.when(odd_node)
            def _():
                up_copy(0, NB, some_other, 0).wait_recv()
                step_ref[...] += in_c[0]

            @pl.when(even)
            def _():
                step_ref[...] += c_ref[0]

            @pl.when(below_top)
            def _():
                up_copy(0, NB, some_other, 1).wait_recv()
                step_ref[...] += in_c[1]

            @pl.when(root)
            def _():
                up_copy(0, NB, some_other, 2).wait_recv()
                step_ref[...] += in_c[2]

            z_ref[1] = step_ref[...]

        pieces = [(k, rows_of(k), slice(B * k, B if k == 0 else W))]
        if k == 1:
            pieces = [(NB + 1, rows_of(0), slice(B, W))] + pieces

        for n, rows, cols in pieces:

            @pl.when(odd_node)
            def _():
                up_copy(0, n, some_other, 0).wait_recv()
                t_ref[1, rows, cols] += in_s[0, rows, cols]

            @pl.when(even)
            def _():
                t_ref[1, rows, cols] += s_ref[0, rows, cols]

            @pl.when(below_top)
            def _():
                up_copy(0, n, some_other, 1).wait_recv()
                t_ref[1, rows, cols] += in_s[1, rows, cols]

            @pl.when(root)
            def _():
                up_copy(0, n, some_other, 2).wait_recv()
                t_ref[1, rows, cols] += in_s[2, rows, cols]

        if k == 1:
            side_ref[...] = t_ref[1, :B, B:2 * B].T

    def eliminate(phase, _):
        sign = jnp.where(phase == 0, 1.0, -1.0).astype(jnp.float32)
        for k in range(NB):
            rows = rows_of(k)
            pl.when(phase == 0)(lambda: arrive(k))
            pl.when(phase == 1)(lambda: receive(k))
            block = t_ref[phase, rows, rows]
            if k > 0:
                before = rows_of(k - 1)
                inv = inv_ref[phase, before, :]
                near = mm(inv, t_ref[phase, before, rows], 1, 0)
                t_ref[phase, before, rows] = near
                block = block - mm(mm(side_ref[...], inv, 1, 1), near, 1, 0)
                col = t_ref[phase, :B * k, rows]
                far = slice(B * k + B, 2 * W)
                t_ref[phase, before, far] = mm(inv, t_ref[phase, before, far], 1, 0)
                t_ref[phase, rows, far] -= mm(col, t_ref[phase, :B * k, far], 0, 0)
                z_ref[phase, :, before] = mm(z_ref[phase, :, before], inv, 1, 1)
                z_ref[phase, :, rows] -= mm(z_ref[phase, :, :B * k], col, 1, 0)
                if k < NB - 1:
                    after = rows_of(k + 1)
                    ahead = t_ref[phase, :B * k, after]
                    t_ref[phase, after, after] -= mm(ahead, ahead, 0, 0)
            if k >= 2:
                for n in range(NB):
                    y = t_ref[phase, (0 if k == 2 else 2 * B):B * k, W:2 * W]
                    base_ref[phase, rows_of(n), B * n:] += sign * mm(
                        y[:, rows_of(n)], y[:, B * n:], 0, 0
                    )
            if k > 0:
                next_cols = slice(B * k + B, B * k + 2 * B)
                side_ref[...] = t_ref[phase, rows, next_cols].T
            inv_ref[phase, rows, :] = inverse_factor(block)
        rows = rows_of(NB - 1)

        target = jnp.where(phase == 0, some_other, parent)
        slot = jnp.where(phase == 0, 1, to_slot)
        sends = jnp.where(phase == 0, odd, below_root)

        def finish(n, cols):
            y = t_ref[phase, rows, W:2 * W]
            r = rows_of(n % (NB + 1))
            s_ref[phase, r, cols] = base_ref[phase, r, cols] + sign * mm(y[:, r], y[:, cols], 0, 0)

        def push(n):
            @pl.when(sends)
            def _():
                up_copy(phase, n, target, slot).start()

        inv = inv_ref[phase, rows, :]

        @pl.when((phase == 0) | below_root)
        def _():
            first = mm(inv, t_ref[phase, rows, W:W + B], 1, 0)
            t_ref[phase, rows, W:W + B] = first
            s_ref[phase, :B, :B] = base_ref[phase, :B, :B] + sign * mm(
                mm(side_ref[...], inv, 1, 1), first, 1, 0
            )
            push(0)
            t_ref[phase, rows, W + B:2 * W] = mm(inv, t_ref[phase, rows, W + B:2 * W], 1, 0)
            finish(NB + 1, slice(B, W))
            push(NB + 1)
            z_ref[phase, :, rows] = mm(z_ref[phase, :, rows], inv, 1, 1)
            c_ref[phase] = g2_ref[phase] + sign * mm(z_ref[phase], t_ref[phase, :, W:2 * W], 1, 0)
            push(NB)
            for n in range(1, NB):
                finish(n, slice(B * n, W))
                push(n)

        @pl.when((phase == 1) & root)
        def _():
            z_ref[1, :, rows] = mm(z_ref[1, :, rows], inv, 1, 1)

        return 0

    lax.fori_loop(0, 2, eliminate, 0)

    @pl.when(below_root)
    def _():
        back(1, W)

        @pl.when(even)
        def _():
            back(0, W)

        down_copy(u_ref, 0, 0, parent).wait_recv()
        step_ref[...] = less_gain(1, u_ref[...])

    @pl.when(root)
    def _():
        back(1, 2 * W)
        step_ref[...] = shift_ref[1]
        down_copy(u_ref, 3, 0, count - 1).start()

    @pl.when(odd_node)
    def _():
        down_copy(u_ref, 0, 0, pos - half).start()
        down_copy(u_ref, 1, 0, pos + half).start()

    @pl.when(odd)
    def _():
        down_copy(f_ref, 2, 1, some_other).wait_recv()

    @pl.when(even)
    def _():
        down_copy(f_ref, 2, 1, some_other).start()
        f_ref[...] = step_ref[...]

    own_ref[...] = step_ref[0:1, :]
    line = unstacked(mm16(stacked(less_gain(0, f_ref[...])), j1_ref[...], 1, 0))
    interior_ref[...] = line[0:1, :] / leaf_prior_ref[0:1, :NI]

    for j in range(1, sub_count):
        leaf_copy(j).wait_send()
        res_copy(j).wait_send()

    @pl.when(odd)
    def _():
        for n in range(NB + 2):
            up_copy(0, n, some_other, 1).wait_send()

    @pl.when(odd_node)
    def _():
        down_copy(u_ref, 0, 0, pos - half).wait_send()
        down_copy(u_ref, 1, 0, pos + half).wait_send()

    @pl.when(root)
    def _():
        down_copy(u_ref, 3, 0, count - 1).wait_send()

    @pl.when(even)
    def _():
        down_copy(f_ref, 2, 1, some_other).wait_send()

    @pl.when(below_root)
    def _():
        for n in range(NB + 2):
            up_copy(1, n, parent, to_slot).wait_send()


def shards(
    sizes,
    measurement_block_rows,
    measurement_residual,
    owner,
    submap_prior_weight,
    separator_measure_rows,
    separator_residual,
    separator_prior_weight,
):
    sub_count = sizes[1]
    block_list, rows_per_block, column_count = measurement_block_rows.shape
    slot_rows = 2 * block_list // sub_count * rows_per_block
    vmem = pl.BlockSpec(memory_space=pltpu.VMEM)
    f32 = jnp.float32
    interior, own = pl.pallas_call(
        lambda *refs: tree_kernel(sizes, *refs),
        out_shape=(
            jax.ShapeDtypeStruct((1, NI), f32),
            jax.ShapeDtypeStruct((1, W), f32),
        ),
        in_specs=[vmem] * 7,
        out_specs=(vmem, vmem),
        scratch_shapes=[
            pltpu.VMEM((2, W, 2 * W), f32),
            pltpu.VMEM((2, W, B), f32),
            pltpu.VMEM((2, W, W), f32),
            pltpu.VMEM((2, 8, W), f32),
            pltpu.VMEM((2, W, W), f32),
            pltpu.VMEM((2, 8, W), f32),
            pltpu.VMEM((3, W, W), f32),
            pltpu.VMEM((3, 8, W), f32),
            pltpu.VMEM((8, W), f32),
            pltpu.VMEM((8, W), f32),
            pltpu.VMEM((8, W), f32),
            pltpu.VMEM((2, 8, W), f32),
            pltpu.VMEM((2, 3, W, W), jnp.bfloat16),
            pltpu.VMEM((sub_count, slot_rows, column_count), jnp.bfloat16),
            pltpu.VMEM((W, NI), jnp.bfloat16),
            pltpu.SemaphoreType.DMA((sub_count,)),
            pltpu.SemaphoreType.DMA((sub_count,)),
            pltpu.SemaphoreType.DMA((2, NB + 2)),
            pltpu.SemaphoreType.DMA((3, NB + 2)),
            pltpu.SemaphoreType.DMA((4,)),
            pltpu.SemaphoreType.DMA((2,)),
            pltpu.SemaphoreType.DMA((3,)),
            pltpu.SemaphoreType.DMA((3,)),
            pltpu.VMEM((sub_count, slot_rows, column_count), jnp.bfloat16),
            pltpu.VMEM((sub_count, 16, B), jnp.bfloat16),
            pltpu.VMEM((sub_count, 16, B), jnp.bfloat16),
            pltpu.SemaphoreType.DMA((sub_count,)),
            pltpu.SemaphoreType.DMA((sub_count,)),
            pltpu.VMEM((2, 8, W), f32),
            pltpu.VMEM((B, B), f32),
        ],
        compiler_params=pltpu.CompilerParams(
            has_side_effects=True, vmem_limit_bytes=56 * 2**20
        ),
    )(
        measurement_block_rows,
        measurement_residual.T,
        owner.T,
        submap_prior_weight,
        separator_measure_rows,
        separator_residual,
        separator_prior_weight,
    )

    def pass_on(a_ref, b_ref, a_out, b_out):
        a_out[...] = a_ref[...]
        b_out[...] = b_ref[...]

    return tuple(pl.pallas_call(
        pass_on,
        out_shape=(jax.ShapeDtypeStruct((1, NI), f32), jax.ShapeDtypeStruct((1, W), f32)),
        in_specs=[vmem] * 2,
        out_specs=(vmem, vmem),
    )(interior, own))


def solution(mesh):
    sizes = (mesh.shape["grp"], mesh.shape["sub"])
    return jax.shard_map(
        lambda *args: shards(sizes, *args),
        mesh=mesh,
        in_specs=(
            P(("grp", "sub"), None, None),
            P(("grp", "sub"), None),
            P(("grp", "sub"), None),
            P(("grp", "sub"), None),
            P(("grp", "sub"), None),
            P(("grp", "sub"), None),
            P(("grp", "sub"), None),
        ),
        out_specs=(P(("grp", "sub"), None), P(("grp", "sub"), None)),
        check_vma=False,
    )
```

```python
import jax
import jax.numpy as jnp
from jax import lax
from jax.experimental import pallas as pl
from jax.experimental.pallas import tpu as pltpu
from jax.sharding import PartitionSpec as P

NI = 1024
W = 512
B = 128
NB = W // B
MESH = pl.DeviceIdType.MESH
highest = lax.Precision.HIGHEST


def mm(a, b, ca, cb):
    return lax.dot_general(
        a, b, (((ca,), (cb,)), ((), ())), precision=highest, preferred_element_type=jnp.float32
    )


def mm16(a, b, ca, cb):
    return lax.dot_general(a, b, (((ca,), (cb,)), ((), ())), preferred_element_type=jnp.float32)


def thirds(x):
    hi = x.astype(jnp.bfloat16)
    rest = x - hi.astype(jnp.float32)
    mid = rest.astype(jnp.bfloat16)
    low = (rest - mid.astype(jnp.float32)).astype(jnp.bfloat16)
    return hi, mid, low


def lane_spread(v, j):
    return jnp.broadcast_to(v[:, j:j + 1], (8, B))


def row_spread(v, i):
    return jnp.broadcast_to(v[i:i + 1, :], (8, B))


def pivot_pair(C, k):
    h, i = k // 8, k % 8
    X, Y = C[h][k], C[h][k + 1]
    a, b, c = row_spread(X, i), row_spread(X, i + 1), row_spread(Y, i + 1)
    r = 1.0 / (a * c - b * b)
    N, M = {}, {}
    for g in range(h, 2):
        Xg, Yg = C[g][k], C[g][k + 1]
        N[g] = (Xg * c - Yg * b, Yg * a - Xg * b)
        M[g] = (N[g][0] * r, N[g][1] * r)
    m = {}
    for j in range(k + 2, 16):
        hj = j // 8
        m[j] = (row_spread(M[hj][0], j % 8), row_spread(M[hj][1], j % 8))
        if j < k + 4:
            x, y = row_spread(C[hj][k], j % 8), row_spread(C[hj][k + 1], j % 8)
            for g in range(hj, 2):
                C[g][j] = C[g][j] - r * (N[g][0] * x + N[g][1] * y)
        else:
            for g in range(hj, 2):
                C[g][j] = C[g][j] - (C[g][k] * m[j][0] + C[g][k + 1] * m[j][1])
    return (a, b, c, r), m


def scaled_rows(u, pairs, sub):
    def join(parts, step):
        total = parts[0]
        for n in range(1, len(parts)):
            total = jnp.where(sub >= n * step, parts[n], total)
        return total

    a, b, r = (join([p[0][n] for p in pairs], 2) for n in (0, 1, 3))
    U, V = join(u, 1), join(u[0::2], 2)
    ra = lax.rsqrt(a)
    d = a * r
    return jnp.where(sub % 2 == 1, (U - (b * (ra * ra)) * V) * (d * lax.rsqrt(d)), U * ra)


def reduce_half(T, off):
    lane = lax.broadcasted_iota(jnp.int32, (8, B), 1)
    sub = lax.broadcasted_iota(jnp.int32, (8, B), 0)
    T = list(T)
    out = []
    n = len(T)
    for t in range(0, n, 2):
        la = off + 8 * t
        C = [[lane_spread(T[t], la + k) for k in range(8)],
             [lane_spread(T[t + 1], la + k) for k in range(16)]]
        cs = {i: [lane_spread(T[i], la + k) for k in range(8)] for i in range(t + 2, n)}
        cs[t + 1] = C[1][:8]
        pairs = [pivot_pair(C, k) for k in range(0, 16, 2)]
        for h in range(2):
            l = la + 8 * h
            inside = (lane >= l) & (lane < l + 8)
            base = jnp.where(inside, jnp.where(lane == sub + l, 1.0, 0.0), T[t + h])
            u = [row_spread(base, k) for k in range(8)]
            four = pairs[4 * h:4 * h + 4]
            for k in range(0, 6, 2):
                for i in range(k + 2, 8):
                    m = four[k // 2][1][i + 8 * h]
                    u[i] = u[i] - (m[0] * u[k] + m[1] * u[k + 1])
            out.append(scaled_rows(u, four, sub))
            if t + h + 1 == n:
                break
            q = [None] * 8
            for k in range(6, -1, -2):
                a, b, c, r = four[k // 2][0]
                q[k] = (c * u[k] - b * u[k + 1]) * r
                q[k + 1] = (a * u[k + 1] - b * u[k]) * r
            for k in range(6, 0, -2):
                for i in range(k):
                    m, m1 = four[i // 2][1][k + 8 * h][i % 2], four[i // 2][1][k + 1 + 8 * h][i % 2]
                    q[i] = q[i] - (m * q[k] + m1 * q[k + 1])
            for i in range(t + h + 1, n):
                if h == 1:
                    cs[i] = [lane_spread(T[i], l + k) for k in range(8)]
                p = [cs[i][k] * q[k] for k in range(8)]
                T[i] = jnp.where(inside, 0.0, T[i]) - (
                    ((p[0] + p[1]) + (p[2] + p[3])) + ((p[4] + p[5]) + (p[6] + p[7])))
    return jnp.concatenate(out, axis=0)


def inverse_factor(D):
    H = B // 2
    lane = lax.broadcasted_iota(jnp.int32, (H, B), 1)
    row = lax.broadcasted_iota(jnp.int32, (H, B), 0)
    top = reduce_half([D[8 * i:8 * i + 8, :] for i in range(H // 8)], 0)
    top = jnp.where((lane >= H) | (lane <= row), top, 0.0)
    low = jnp.where(lane < H, 0.0, D[H:, :]) - mm(top[:, H:], top, 0, 0)
    low = reduce_half([low[8 * i:8 * i + 8, :] for i in range(H // 8)], H)
    return jnp.concatenate(
        [jnp.where(lane < H, top, 0.0), jnp.where(lane <= row + H, low, 0.0)], axis=0)


def add_diag(square, row):
    r = lax.broadcasted_iota(jnp.int32, square.shape, 0)
    c = lax.broadcasted_iota(jnp.int32, square.shape, 1)
    return square + jnp.where(r == c, row, 0.0)


def tree_kernel(
    sizes, blocks_ref, block_res_ref, owner_ref, leaf_prior_ref, node_rows_any, node_res_ref, node_prior_ref,
    interior_ref, own_ref,
    t_ref, inv_ref, base_ref, g2_ref, s_ref, c_ref, in_s, in_c, step_ref, u_ref, f_ref,
    shift_ref, gain_ref, land_ref, j1_ref, leaf_send, leaf_recv, up_send, up_recv, down_send, down_recv,
    early_send, early_recv, rows_ref, res_ref, land_res_ref, res_send, res_recv, z_ref, side_ref, node_rows_ref, node_sem,
):
    grp_count, sub_count = sizes
    count = grp_count * sub_count
    depth = count.bit_length() - 1
    pos = lax.axis_index("grp") * sub_count + lax.axis_index("sub")
    odd = pos % 2 == 1
    even = pos % 2 == 0
    node_copy = pltpu.make_async_copy(node_rows_any, node_rows_ref, node_sem)
    node_copy.start()
    middle = count // 2 - 1
    top = pos == count - 1
    root = pos == middle
    below_root = pos != middle
    odd_node = odd & (pos != count - 1)
    below_top = pos != count - 1
    stride = jnp.int32(0)
    left = jnp.int32(0)
    for level in range(1, depth + 2):
        here = jnp.where((pos + 1) % 2**level == 2 ** (level - 1), 1, 0)
        stride = stride + here * 2 ** (level - 1)
        left = left + here * (1 - (pos + 1) // 2**level % 2)
    parent = jnp.where(top, middle, pos + (2 * left - 1) * stride)
    parent = jnp.where(root, count - 1, parent)
    to_slot = jnp.where(top, 2, 1 - left)
    half = stride // 2

    def device(target):
        return (target // sub_count, target % sub_count)

    def up_copy(phase, n, target, slot):
        if n == NB:
            src, dst = c_ref.at[phase], in_c.at[slot]
        else:
            at = (pl.ds(B * n, B), pl.ds(B * n, W - B * n))
            if n == 0:
                at = (pl.ds(0, B), pl.ds(0, B))
            if n == NB + 1:
                at = (pl.ds(0, B), pl.ds(B, W - B))
            src, dst = s_ref.at[phase, at[0], at[1]], in_s.at[slot, at[0], at[1]]
        return pltpu.make_async_remote_copy(
            src_ref=src, dst_ref=dst, send_sem=up_send.at[phase, n],
            recv_sem=up_recv.at[slot, n], device_id=device(target), device_id_type=MESH)

    def down_copy(dst, n, r, target):
        return pltpu.make_async_remote_copy(
            src_ref=step_ref, dst_ref=dst, send_sem=down_send.at[n], recv_sem=down_recv.at[r],
            device_id=device(target), device_id_type=MESH)

    def early_copy(n):
        src = (base_ref.at[1], t_ref.at[1, :, pl.ds(W, W)], g2_ref.at[1])[n]
        dst = (in_s.at[0], in_s.at[2], in_c.at[0])[n]
        return pltpu.make_async_remote_copy(
            src_ref=src, dst_ref=dst, send_sem=early_send.at[n], recv_sem=early_recv.at[n],
            device_id=device(jnp.where(root, count - 1, middle)), device_id_type=MESH)

    some_other = jnp.where(odd, pos - 1, pos + 1)

    def rows_of(k):
        return slice(B * k, B * k + B)

    group = lax.axis_index("grp")
    place = lax.axis_index("sub")
    slot_rows = 2 * blocks_ref.shape[0] // sub_count * blocks_ref.shape[1]
    per_block = B // slot_rows

    def peer_of(j):
        peer = place
        for bit in range(sub_count.bit_length() - 1):
            if j >> bit & 1:
                peer = peer + 2**bit * (1 - 2 * (place // 2**bit % 2))
        return peer

    def leaf_copy(j):
        peer = peer_of(j)
        return pltpu.make_async_remote_copy(
            src_ref=rows_ref.at[peer], dst_ref=land_ref.at[j], send_sem=leaf_send.at[j],
            recv_sem=leaf_recv.at[j], device_id=(group, peer), device_id_type=MESH)

    def res_copy(j):
        return pltpu.make_async_remote_copy(
            src_ref=res_ref.at[j], dst_ref=land_res_ref.at[j], send_sem=res_send.at[j],
            recv_sem=res_recv.at[j], device_id=(group, peer_of(j)), device_id_type=MESH)

    block_list, per, columns = blocks_ref.shape
    held = block_list * per
    f32, bf16 = jnp.float32, jnp.bfloat16

    def grid(shape, dim):
        return lax.broadcasted_iota(jnp.int32, shape, dim)

    def many(row):
        return jnp.broadcast_to(row, (16, row.shape[1])).astype(bf16)

    repeat = jnp.where(
        grid((block_list, held), 1) // per == grid((block_list, held), 0), 1.0, 0.0
    ).astype(bf16)
    earlier = jnp.where(
        grid((block_list, block_list), 0) < grid((block_list, block_list), 1), 1.0, 0.0
    ).astype(bf16)
    kinds = max(sub_count, 16)
    names = jnp.where(grid((kinds, block_list), 0) == owner_ref[0:1, :], 1.0, 0.0)
    ahead_of = jnp.sum(mm16(names.astype(bf16), earlier, 1, 0) * names, axis=0, keepdims=True)
    rank = mm16(many(ahead_of), repeat, 1, 0)[0:1, :]
    named = mm16(many(owner_ref[0:1, :].astype(f32)), repeat, 1, 0)[0:1, :]
    at_row = (rank * per).astype(jnp.int32) + grid((1, held), 1) % per
    named = named.astype(jnp.int32)
    spread = mm16(
        jnp.concatenate([block_res_ref[...].astype(f32), jnp.zeros((16 - per, block_list), f32)], axis=0).astype(bf16),
        repeat, 1, 0,
    )
    spread = jnp.where(grid((16, held), 0) == grid((16, held), 1) % per, spread, 0.0)
    line_res = many(jnp.sum(spread, axis=0, keepdims=True))
    for j in range(sub_count):
        hit = grid((B, held), 0) == at_row + (j % per_block) * slot_rows
        hit = jnp.where(hit & (named == peer_of(j)), 1.0, 0.0).astype(bf16)
        res_ref[j] = mm16(line_res, hit, 1, 1).astype(bf16)
        if j > 0:
            res_copy(j).start()

    table = jnp.where(
        grid((sub_count * slot_rows, held), 0) == named * slot_rows + at_row, 1.0, 0.0
    ).astype(bf16)
    placed = mm16(table, blocks_ref[...].reshape(held, columns), 1, 0)
    for n in range(sub_count):
        rows_ref[n] = placed[slot_rows * n:slot_rows * (n + 1), :].astype(bf16)
    for j in range(1, sub_count):
        leaf_copy(j).start()

    def arrive(k):
        rows = rows_of(k)
        parts = []
        values = jnp.zeros((16, B), f32)
        for j in range(per_block * k, per_block * k + per_block):
            if j == 0:
                parts.append(rows_ref[place].astype(f32))
                values = values + res_ref[0].astype(f32)
            else:
                leaf_copy(j).wait_recv()
                res_copy(j).wait_recv()
                parts.append(land_ref[j].astype(f32))
                values = values + land_res_ref[j].astype(f32)
        block = jnp.concatenate(parts, axis=0)
        t_ref[0, rows, W:2 * W] = block[:, NI:]
        z_ref[0, :, rows] = values[0:8, :]
        line = block[:, :NI]
        j1_ref[rows, :] = line.astype(jnp.bfloat16)
        above = j1_ref[:B * k + B, :]
        scaled = thirds(line * (1.0 / leaf_prior_ref[0:1, :NI]))
        square = mm16(above, scaled[2], 1, 1) + mm16(above, scaled[1], 1, 1)
        square = square + mm16(above, scaled[0], 1, 1)
        for i in range(k):
            part = square[rows_of(i), :]
            if i > 0:
                part = part - mm(t_ref[0, :B * i, rows_of(i)], t_ref[0, :B * i, rows], 0, 0)
            if i < k - 1:
                part = mm(inv_ref[0, rows_of(i), :], part, 1, 0)
            t_ref[0, rows_of(i), rows] = part
            if i == k - 1:
                side_ref[...] = part.T
        corner = add_diag(square[rows, :], jnp.float32(1.0))
        if k > 1:
            corner = corner - mm(t_ref[0, :B * k - B, rows], t_ref[0, :B * k - B, rows], 0, 0)
        t_ref[0, rows, rows] = corner

    node_copy.wait()
    r1 = node_rows_ref[:, :W]
    r2 = node_rows_ref[:, W:]
    res = jnp.broadcast_to(node_res_ref[0:1, :], (16, node_res_ref.shape[1]))
    t_ref[1, :, :W] = add_diag(mm16(r1, r1, 0, 0), node_prior_ref[0:1, :W])

    @pl.when(root)
    def _():
        t_ref[1, :, W:2 * W] = mm16(r2, r1, 0, 0)

    @pl.when(below_root)
    def _():
        t_ref[1, :, W:2 * W] = mm16(r1, r2, 0, 0)

    base_ref[1] = jnp.where(top, 0.0, add_diag(mm16(r2, r2, 0, 0), node_prior_ref[0:1, W:]))
    step_ref[...] = mm16(res, r1, 1, 0)[0:8, :]
    g2_ref[1] = jnp.where(top, 0.0, mm16(res, r2, 1, 0)[0:8, :])

    @pl.when(root)
    def _():
        for n in range(3):
            early_copy(n).start()

    t_ref[0, :, :W] = jnp.zeros((W, W), jnp.float32)
    base_ref[0] = add_diag(jnp.zeros((W, W), jnp.float32), leaf_prior_ref[0:1, NI:])
    g2_ref[0] = jnp.zeros((8, W), jnp.float32)

    def back(phase, first):
        for k in range(NB - 1, -1, -1):
            line = z_ref[phase, :, rows_of(k)]
            rest = slice(B * k + B, W)
            if k < NB - 1:
                line = line - mm(shift_ref[phase, :, rest], t_ref[phase, rows_of(k), rest], 1, 1)
            shift_ref[phase, :, rows_of(k)] = mm(line, inv_ref[phase, rows_of(k), :], 1, 0)
            if first < 2 * W:
                right = t_ref[phase, rows_of(k), first:]
                if k < NB - 1:
                    right = right - mm(
                        t_ref[phase, rows_of(k), rest], t_ref[phase, rest, first:], 1, 0
                    )
                t_ref[phase, rows_of(k), first:] = mm(inv_ref[phase, rows_of(k), :], right, 0, 0)
        if first < 2 * W:
            for n, part in enumerate(thirds(t_ref[phase, :, W:2 * W].T)):
                gain_ref[phase, n] = part

    def stacked(row):
        return jnp.concatenate([x for x in thirds(jnp.concatenate([row, row], axis=0))], axis=0)

    def unstacked(total):
        return total[32:40] + total[16:24] + total[0:8]

    def less_gain(phase, row):
        stack = stacked(row)
        total = mm16(stack, gain_ref[phase, 2], 1, 0) + mm16(stack, gain_ref[phase, 1], 1, 0)
        total = total + mm16(stack, gain_ref[phase, 0], 1, 0)
        return shift_ref[phase] - unstacked(total)

    def receive(k):
        if k == 0:

            @pl.when(odd)
            def _():
                back(0, W)

            @pl.when(root)
            def _():
                for n in range(3):
                    early_copy(n).wait_send()

            @pl.when(top)
            def _():
                for n in range(3):
                    early_copy(n).wait_recv()
                step_ref[...] += in_c[0]
                t_ref[1, :, :W] += in_s[0]
                t_ref[1, :, W:2 * W] = in_s[2]

        if k == 1:

            @pl.when(odd_node)
            def _():
                up_copy(0, NB, some_other, 0).wait_recv()
                step_ref[...] += in_c[0]

            @pl.when(even)
            def _():
                step_ref[...] += c_ref[0]

            @pl.when(below_top)
            def _():
                up_copy(0, NB, some_other, 1).wait_recv()
                step_ref[...] += in_c[1]

            @pl.when(root)
            def _():
                up_copy(0, NB, some_other, 2).wait_recv()
                step_ref[...] += in_c[2]

            z_ref[1] = step_ref[...]

        pieces = [(k, rows_of(k), slice(B * k, B if k == 0 else W))]
        if k == 1:
            pieces = [(NB + 1, rows_of(0), slice(B, W))] + pieces

        for n, rows, cols in pieces:

            @pl.when(odd_node)
            def _():
                up_copy(0, n, some_other, 0).wait_recv()
                t_ref[1, rows, cols] += in_s[0, rows, cols]

            @pl.when(even)
            def _():
                t_ref[1, rows, cols] += s_ref[0, rows, cols]

            @pl.when(below_top)
            def _():
                up_copy(0, n, some_other, 1).wait_recv()
                t_ref[1, rows, cols] += in_s[1, rows, cols]

            @pl.when(root)
            def _():
                up_copy(0, n, some_other, 2).wait_recv()
                t_ref[1, rows, cols] += in_s[2, rows, cols]

        if k == 1:
            side_ref[...] = t_ref[1, :B, B:2 * B].T

    def eliminate(phase, _):
        sign = jnp.where(phase == 0, 1.0, -1.0).astype(jnp.float32)
        for k in range(NB):
            rows = rows_of(k)
            pl.when(phase == 0)(lambda: arrive(k))
            pl.when(phase == 1)(lambda: receive(k))
            block = t_ref[phase, rows, rows]
            if k > 0:
                before = rows_of(k - 1)
                inv = inv_ref[phase, before, :]
                near = mm(inv, t_ref[phase, before, rows], 1, 0)
                t_ref[phase, before, rows] = near
                block = block - mm(mm(side_ref[...], inv, 1, 1), near, 1, 0)
                col = t_ref[phase, :B * k, rows]
                far = slice(B * k + B, 2 * W)
                t_ref[phase, before, far] = mm(inv, t_ref[phase, before, far], 1, 0)
                t_ref[phase, rows, far] -= mm(col, t_ref[phase, :B * k, far], 0, 0)
                z_ref[phase, :, before] = mm(z_ref[phase, :, before], inv, 1, 1)
                z_ref[phase, :, rows] -= mm(z_ref[phase, :, :B * k], col, 1, 0)
                if k < NB - 1:
                    after = rows_of(k + 1)
                    ahead = t_ref[phase, :B * k, after]
                    t_ref[phase, after, after] -= mm(ahead, ahead, 0, 0)
            if k >= 2:
                for n in range(NB):
                    y = t_ref[phase, (0 if k == 2 else 2 * B):B * k, W:2 * W]
                    base_ref[phase, rows_of(n), B * n:] += sign * mm(
                        y[:, rows_of(n)], y[:, B * n:], 0, 0
                    )
            if k > 0:
                next_cols = slice(B * k + B, B * k + 2 * B)
                side_ref[...] = t_ref[phase, rows, next_cols].T
            inv_ref[phase, rows, :] = inverse_factor(block)
        rows = rows_of(NB - 1)

        target = jnp.where(phase == 0, some_other, parent)
        slot = jnp.where(phase == 0, 1, to_slot)
        sends = jnp.where(phase == 0, odd, below_root)

        def finish(n, cols):
            y = t_ref[phase, rows, W:2 * W]
            r = rows_of(n % (NB + 1))
            s_ref[phase, r, cols] = base_ref[phase, r, cols] + sign * mm(y[:, r], y[:, cols], 0, 0)

        def push(n):
            @pl.when(sends)
            def _():
                up_copy(phase, n, target, slot).start()

        inv = inv_ref[phase, rows, :]

        @pl.when((phase == 0) | below_root)
        def _():
            first = mm(inv, t_ref[phase, rows, W:W + B], 1, 0)
            t_ref[phase, rows, W:W + B] = first
            s_ref[phase, :B, :B] = base_ref[phase, :B, :B] + sign * mm(
                mm(side_ref[...], inv, 1, 1), first, 1, 0
            )
            push(0)
            t_ref[phase, rows, W + B:2 * W] = mm(inv, t_ref[phase, rows, W + B:2 * W], 1, 0)
            finish(NB + 1, slice(B, W))
            push(NB + 1)
            z_ref[phase, :, rows] = mm(z_ref[phase, :, rows], inv, 1, 1)
            c_ref[phase] = g2_ref[phase] + sign * mm(z_ref[phase], t_ref[phase, :, W:2 * W], 1, 0)
            push(NB)
            for n in range(1, NB):
                finish(n, slice(B * n, W))
                push(n)

        @pl.when((phase == 1) & root)
        def _():
            z_ref[1, :, rows] = mm(z_ref[1, :, rows], inv, 1, 1)

        return 0

    lax.fori_loop(0, 2, eliminate, 0)

    @pl.when(below_root)
    def _():
        back(1, W)

        @pl.when(even)
        def _():
            back(0, W)

        down_copy(u_ref, 0, 0, parent).wait_recv()
        step_ref[...] = less_gain(1, u_ref[...])

    @pl.when(root)
    def _():
        back(1, 2 * W)
        step_ref[...] = shift_ref[1]
        down_copy(u_ref, 3, 0, count - 1).start()

    @pl.when(odd_node)
    def _():
        down_copy(u_ref, 0, 0, pos - half).start()
        down_copy(u_ref, 1, 0, pos + half).start()

    @pl.when(odd)
    def _():
        down_copy(f_ref, 2, 1, some_other).wait_recv()

    @pl.when(even)
    def _():
        down_copy(f_ref, 2, 1, some_other).start()
        f_ref[...] = step_ref[...]

    own_ref[...] = step_ref[0:1, :]
    line = unstacked(mm16(stacked(less_gain(0, f_ref[...])), j1_ref[...], 1, 0))
    interior_ref[...] = line[0:1, :] / leaf_prior_ref[0:1, :NI]

    for j in range(1, sub_count):
        leaf_copy(j).wait_send()
        res_copy(j).wait_send()

    @pl.when(odd)
    def _():
        for n in range(NB + 2):
            up_copy(0, n, some_other, 1).wait_send()

    @pl.when(odd_node)
    def _():
        down_copy(u_ref, 0, 0, pos - half).wait_send()
        down_copy(u_ref, 1, 0, pos + half).wait_send()

    @pl.when(root)
    def _():
        down_copy(u_ref, 3, 0, count - 1).wait_send()

    @pl.when(even)
    def _():
        down_copy(f_ref, 2, 1, some_other).wait_send()

    @pl.when(below_root)
    def _():
        for n in range(NB + 2):
            up_copy(1, n, parent, to_slot).wait_send()


def shards(
    sizes,
    measurement_block_rows,
    measurement_residual,
    owner,
    submap_prior_weight,
    separator_measure_rows,
    separator_residual,
    separator_prior_weight,
):
    sub_count = sizes[1]
    block_list, rows_per_block, column_count = measurement_block_rows.shape
    slot_rows = 2 * block_list // sub_count * rows_per_block
    vmem = pl.BlockSpec(memory_space=pltpu.VMEM)
    f32 = jnp.float32
    interior, own = pl.pallas_call(
        lambda *refs: tree_kernel(sizes, *refs),
        out_shape=(
            jax.ShapeDtypeStruct((1, NI), f32),
            jax.ShapeDtypeStruct((1, W), f32),
        ),
        in_specs=[vmem] * 4 + [pl.BlockSpec(memory_space=pl.ANY)] + [vmem] * 2,
        out_specs=(vmem, vmem),
        scratch_shapes=[
            pltpu.VMEM((2, W, 2 * W), f32),
            pltpu.VMEM((2, W, B), f32),
            pltpu.VMEM((2, W, W), f32),
            pltpu.VMEM((2, 8, W), f32),
            pltpu.VMEM((2, W, W), f32),
            pltpu.VMEM((2, 8, W), f32),
            pltpu.VMEM((3, W, W), f32),
            pltpu.VMEM((3, 8, W), f32),
            pltpu.VMEM((8, W), f32),
            pltpu.VMEM((8, W), f32),
            pltpu.VMEM((8, W), f32),
            pltpu.VMEM((2, 8, W), f32),
            pltpu.VMEM((2, 3, W, W), jnp.bfloat16),
            pltpu.VMEM((sub_count, slot_rows, column_count), jnp.bfloat16),
            pltpu.VMEM((W, NI), jnp.bfloat16),
            pltpu.SemaphoreType.DMA((sub_count,)),
            pltpu.SemaphoreType.DMA((sub_count,)),
            pltpu.SemaphoreType.DMA((2, NB + 2)),
            pltpu.SemaphoreType.DMA((3, NB + 2)),
            pltpu.SemaphoreType.DMA((4,)),
            pltpu.SemaphoreType.DMA((2,)),
            pltpu.SemaphoreType.DMA((3,)),
            pltpu.SemaphoreType.DMA((3,)),
            pltpu.VMEM((sub_count, slot_rows, column_count), jnp.bfloat16),
            pltpu.VMEM((sub_count, 16, B), jnp.bfloat16),
            pltpu.VMEM((sub_count, 16, B), jnp.bfloat16),
            pltpu.SemaphoreType.DMA((sub_count,)),
            pltpu.SemaphoreType.DMA((sub_count,)),
            pltpu.VMEM((2, 8, W), f32),
            pltpu.VMEM((B, B), f32),
            pltpu.VMEM(separator_measure_rows.shape, jnp.bfloat16),
            pltpu.SemaphoreType.DMA,
        ],
        compiler_params=pltpu.CompilerParams(
            has_side_effects=True, vmem_limit_bytes=56 * 2**20
        ),
    )(
        measurement_block_rows,
        measurement_residual.T,
        owner.T,
        submap_prior_weight,
        separator_measure_rows,
        separator_residual,
        separator_prior_weight,
    )

    def pass_on(a_ref, b_ref, a_out, b_out):
        a_out[...] = a_ref[...]
        b_out[...] = b_ref[...]

    return tuple(pl.pallas_call(
        pass_on,
        out_shape=(jax.ShapeDtypeStruct((1, NI), f32), jax.ShapeDtypeStruct((1, W), f32)),
        in_specs=[vmem] * 2,
        out_specs=(vmem, vmem),
    )(interior, own))


def solution(mesh):
    sizes = (mesh.shape["grp"], mesh.shape["sub"])
    return jax.shard_map(
        lambda *args: shards(sizes, *args),
        mesh=mesh,
        in_specs=(
            P(("grp", "sub"), None, None),
            P(("grp", "sub"), None),
            P(("grp", "sub"), None),
            P(("grp", "sub"), None),
            P(("grp", "sub"), None),
            P(("grp", "sub"), None),
            P(("grp", "sub"), None),
        ),
        out_specs=(P(("grp", "sub"), None), P(("grp", "sub"), None)),
        check_vma=False,
    )
```
